32 devices in a mesh: dp: 16 (over z, y, x), mp: 2 (over core).
Axes of the slice: x: 2, y: 2, z: 4, core: 2. Of those that a mesh axis runs over, the one named last changes fastest.
Arguments:
- value_grads: bfloat16 [16, 24, 128, 128], P('dp', 'mp'), may hold values from -2 to 2
- key_grads: bfloat16 [16, 2, 16, 128, 128], P('dp', 'mp'), may hold values from -0.75 to 0.75
- owners: int32 [40, 1], P('mp'), may hold values from 0 to 15; in each aligned block of 20 rows (0 to 19, 20 to 39, ...) at most 2 rows name the same one
- weights: float32 [16, 2, 2, 128, 128], P('dp', 'mp'), may hold values from -6 to 6
- left: float32 [16, 2, 2, 128, 128], P('dp', 'mp'), may hold values from -0.25 to 4, as said below
- right: float32 [16, 2, 2, 128, 128], P('dp', 'mp'), may hold values from -0.25 to 4, as said below
- left_root: float32 [16, 2, 2, 128, 128], P('dp', 'mp'), may hold values from -0.25 to 4
- right_root: float32 [16, 2, 2, 128, 128], P('dp', 'mp'), may hold values from -0.25 to 4
- second: float32 [16, 2, 2, 128, 128], P('dp', 'mp'), may hold values from 0.001 to 0.1
Outputs:
- new_weights: float32 [16, 2, 2, 128, 128], P('dp', 'mp')
- new_left: float32 [16, 2, 2, 128, 128], P('dp', 'mp')
- new_right: float32 [16, 2, 2, 128, 128], P('dp', 'mp')
- new_second: float32 [16, 2, 2, 128, 128], P('dp', 'mp')
- new_values: bfloat16 [24, 128, 128], P('mp')
- new_keys: bfloat16 [16, 128, 128], P('mp')
The draws below stay inside these ranges and needn't reach their ends.
Inputs may be any that keep to these rules, and one draw needn't show every extreme that they name: `owners`: within each aligned block of 20 rows (one index of mp) no dp index appears more than 2 times; some appears exactly 2 times. `left`: Symmetric. `right`: Symmetric.
All inputs are finite; a program needn't handle non-finite values.
Results may differ from the reference program's by a relative error of at most 0.0035.
Values may be sent and summed in bfloat16 or wider, within the bound.
A program may use at most 64 MiB of HBM per device.

```python
import math
import jax
import jax.numpy as jnp
import numpy as np
from jax import lax

B = 128
CAP = 2
KEYB = 16
NBM = 12
VBLOCKS = 24
KBM = 8
ALLB = 20
N_DP = 16
N_MP = 2


def symmetric_draw(key):
    first, other = jax.random.split(key)
    shape = (N_DP, N_MP, CAP, B, B)
    raw = jax.random.truncated_normal(first, -4.0, 4.0, shape, jnp.float32)
    offdiag = jnp.clip((raw + jnp.swapaxes(raw, -1, -2)) * (0.35 / math.sqrt(B)), -0.25, 0.25)
    diagonal = jax.random.uniform(other, shape[:-1], jnp.float32, 0.5, 2.0)
    identity = jnp.eye(B, dtype=jnp.float32)
    return offdiag * (1.0 - identity) + identity * diagonal[..., None]


def draw_left(key, part):
    return symmetric_draw(jax.random.fold_in(key, 11))


def draw_right(key, part):
    return symmetric_draw(jax.random.fold_in(key, 23))


def draw_left_root(key, part):
    return symmetric_draw(jax.random.fold_in(key, 37))


def draw_right_root(key, part):
    return symmetric_draw(jax.random.fold_in(key, 41))


def shard_levels(own_key, dims, pieces, least, high):
    gain = 1.0
    for dim, parts in pieces:
        draws = jax.random.uniform(jax.random.fold_in(jax.random.fold_in(own_key, 6), dim), (parts,), jnp.float32, least / len(pieces), high / len(pieces))
        gain = gain * jnp.repeat(jnp.exp(draws), dims[dim] // parts).reshape((-1,) + (1,) * (len(dims) - 1 - dim))
    return gain


def routed_block(stream_key, own, number, rows, number_of, top, limit, lean):
    order = jax.random.permutation(stream_key, number_of)
    heavy_load, common = portions_of(number_of, rows * top, limit, lean, True), portions_of(number_of, rows * top, limit, lean, False)
    places = jnp.arange(number_of)

    def named(lengths, turn):
        used = int((lengths > 0).sum())
        fixed = max(1, used // 4)
        passed = fixed + (places - fixed + turn * (used - fixed)) % max(1, number_of - fixed)
        return jnp.zeros((number_of,), jnp.int32).at[order[jnp.where(places < fixed, places, passed)]].set(jnp.asarray(lengths, jnp.int32))

    lengths = jnp.where(number % 4 == 0, named(heavy_load, number // 4), named(common, number - number // 4 - 1))
    mixed = jax.random.permutation(jax.random.fold_in(own, 3), number_of)
    giver, taker = mixed[0:number_of // 2 * 2:2], mixed[1:number_of // 2 * 2:2]
    room = jnp.minimum(lengths[giver] - 1, limit - lengths[taker]) // 2
    room = jnp.where((giver == order[0]) | (taker == order[0]) | (lengths[taker] == 0), 0, jnp.maximum(room, 0))
    passed = jax.random.randint(jax.random.fold_in(own, 4), (number_of // 2,), 0, 1 << 20) % (room + 1)
    lengths = lengths.at[giver].add(-passed).at[taker].add(passed)
    labels = jnp.searchsorted(jnp.cumsum(lengths), jnp.arange(rows * top), side="right").astype(jnp.int32)
    grid = labels.reshape(top, rows).T
    grid = grid[jax.random.permutation(jax.random.fold_in(own, 1), rows)]
    turn = jax.random.randint(jax.random.fold_in(own, 2), (rows, 1), 0, top)
    return jnp.take_along_axis(grid, (jnp.arange(top)[None, :] + turn) % top, axis=1)


def portions_of(amount, total, most, skew, full):
    loads = [(1 << 20) // math.isqrt(grade ** skew) + 1 for grade in range(1, amount + 1)]
    largest = most if full else min(most, max(-(-total // amount), total * loads[0] // sum(loads)))
    least = 1 if total - largest >= amount - 1 else 0
    given, rest = [largest] + [least] * (amount - 1), total - largest - least * (amount - 1)
    while rest > 0:
        candidates = [i for i in range(1, amount) if given[i] < largest] or [i for i in range(1, amount) if given[i] < most]
        pool, remaining = sum([loads[i] for i in candidates]), rest
        for i in candidates:
            extra = min(most - given[i], max(1, remaining * loads[i] // pool), rest)
            given[i] = given[i] + extra
            rest = rest - extra
    return np.array(given)


def centred(key, dims, width, reach, shards=(), kind=jnp.bfloat16):
    values = jax.random.normal(key, dims, jnp.float32) * width
    if len(shards) > 0:
        values = shard_levels(key, dims, shards, -0.22, 0.18) * values
    return jnp.clip(values, min=-reach, max=reach).astype(kind)


def setup_inputs(seed: int = 0) -> dict:
    splits = jax.random.split(jax.random.key(seed), 10)
    value_grads = centred(splits[0], (N_DP, VBLOCKS, B, B), 0.125, 2.0, ((0, 16), (1, 2)))
    key_grads = centred(splits[1], (N_DP, N_MP, KEYB, B, B), 0.05, 0.75, ((0, 16), (1, 2)))
    owners_keys = jax.random.split(jax.random.fold_in(splits[2], 1), (N_MP * ALLB) // ALLB)
    owners_turns = jax.random.permutation(jax.random.fold_in(splits[2], 3), (N_MP * ALLB) // ALLB)
    owners = jax.vmap(lambda own, number: routed_block(jax.random.fold_in(splits[2], 2), own, number, ALLB, N_DP, 1, CAP, 2))(owners_keys, owners_turns).reshape((N_MP * ALLB, 1))
    weights = centred(splits[3], (N_DP, N_MP, CAP, B, B), 1.0, 6.0, ((0, 16), (1, 2)), jnp.float32)
    left = draw_left(jax.random.fold_in(splits[9], 71), 0)
    right = draw_right(jax.random.fold_in(splits[9], 71), 0)
    left_root = draw_left_root(jax.random.fold_in(splits[9], 71), 0)
    right_root = draw_right_root(jax.random.fold_in(splits[9], 71), 0)
    second = jnp.clip(jnp.exp(math.log(0.1) - 4.6051702 * jax.random.uniform(splits[8], (N_DP, N_MP, CAP, B, B), jnp.float32) ** shard_levels(splits[8], (N_DP, N_MP, CAP, B, B), ((0, 16), (1, 2)), -0.2, 0.2)), 0.001, 0.1)
    return {"value_grads": value_grads, "key_grads": key_grads, "owners": owners, "weights": weights, "left": left, "right": right, "left_root": left_root, "right_root": right_root, "second": second}


STAT_DECAY = 0.95
ADAM_DECAY = 0.95
LEARN_RATE = 0.1
NORM_EPS = 1e-06

def slot_onehot(owner_ids, slot_count):
    position = jnp.arange(owner_ids.shape[0], dtype=jnp.int32)
    same_owner = owner_ids[:, None] == owner_ids[None, :]
    earlier = position[None, :] < position[:, None]
    slot_rank = lax.optimization_barrier(jnp.sum((same_owner & earlier).astype(jnp.int32), axis=1))
    target = owner_ids * CAP + slot_rank
    return (target[:, None] == jnp.arange(slot_count, dtype=jnp.int32)[None, :]).astype(jnp.float32)

def shampoo(gradient, weights, left, right, left_root, right_root, second):
    high = lax.Precision.HIGHEST
    new_left = STAT_DECAY * left + (1.0 - STAT_DECAY) * jnp.einsum('...ij,...kj->...ik', gradient, gradient, precision=high)
    new_right = STAT_DECAY * right + (1.0 - STAT_DECAY) * jnp.einsum('...ji,...jk->...ik', gradient, gradient, precision=high)
    shaped = jnp.einsum('...ij,...jk->...ik', left_root, gradient, precision=high)
    shaped = jnp.einsum('...ij,...jk->...ik', shaped, right_root, precision=high)
    new_second = ADAM_DECAY * second + (1.0 - ADAM_DECAY) * gradient * gradient
    adam_step = gradient / jnp.sqrt(new_second)
    adam_norm = jnp.sqrt(lax.optimization_barrier(jnp.sum(adam_step * adam_step, axis=(-2, -1), keepdims=True)))
    shaped_norm = jnp.sqrt(lax.optimization_barrier(jnp.sum(shaped * shaped, axis=(-2, -1), keepdims=True)))
    graft_scale = adam_norm / (shaped_norm + NORM_EPS)
    new_weights = weights - LEARN_RATE * graft_scale * shaped
    return (new_weights, new_left, new_right, new_second)

def reference(value_grads, key_grads, owners, weights, left, right, left_root, right_root, second):
    high = lax.Precision.HIGHEST
    slot_count = N_DP * CAP
    value_total = lax.optimization_barrier(jnp.sum(value_grads, axis=0, dtype=jnp.float32))
    key_partial = lax.optimization_barrier(jnp.sum(key_grads, axis=1, dtype=jnp.float32)).astype(jnp.bfloat16)
    key_total = lax.optimization_barrier(jnp.sum(key_partial, axis=0, dtype=jnp.float32))
    tables = []
    gathered = []
    for shard in range(N_MP):
        blocks = jnp.concatenate([value_total[shard * NBM:(shard + 1) * NBM], key_total[shard * KBM:(shard + 1) * KBM]], axis=0)
        one_hot = slot_onehot(owners[shard * ALLB:(shard + 1) * ALLB, 0], slot_count)
        tables.append(one_hot)
        placed = jnp.einsum('bj,bxy->jxy', one_hot, blocks, precision=high)
        gathered.append(placed.reshape(N_DP, CAP, B, B))
    gradient = jnp.stack(gathered, axis=1)
    new_weights, new_left, new_right, new_second = shampoo(gradient, weights, left, right, left_root, right_root, second)
    rounded = new_weights.astype(jnp.bfloat16)
    value_list = []
    key_list = []
    for shard in range(N_MP):
        flat_new = rounded[:, shard].reshape(slot_count, B, B).astype(jnp.float32)
        picked = jnp.einsum('bj,jxy->bxy', tables[shard], flat_new, precision=high).astype(jnp.bfloat16)
        value_list.append(picked[:NBM])
        key_list.append(picked[NBM:])
    new_values = jnp.concatenate(value_list, axis=0)
    new_keys = jnp.concatenate(key_list, axis=0)
    return (new_weights, new_left, new_right, new_second, new_values, new_keys)
```

```python
import functools

import jax
import jax.numpy as jnp
from jax import lax
from jax.experimental import pallas as pl
from jax.experimental.pallas import tpu as pltpu
from jax.sharding import PartitionSpec as P

STAT_DECAY = 0.95
ADAM_DECAY = 0.95
LEARN_RATE = 0.1
NORM_EPS = 1e-06
MESH = pl.DeviceIdType.MESH
HIGH = lax.Precision.HIGHEST


def dot(a, b, contract):
    return lax.dot_general(
        a, b, ((contract[0], contract[1]), ((), ())), precision=HIGH, preferred_element_type=jnp.float32
    )


def main_kernel(
    dims,
    owners,
    value_hbm,
    key_hbm,
    weights_hbm,
    left_hbm,
    right_hbm,
    lroot_hbm,
    rroot_hbm,
    second_hbm,
    out_weights,
    out_left,
    out_right,
    out_second,
    gathered,
    table,
    blocks,
    key_mine,
    key_recv,
    weights,
    left,
    right,
    lroot,
    rroot,
    second,
    send1,
    recv1,
    send2,
    recv2,
    acc,
    send3,
    recv3,
    grad,
    shaped,
    load_sem,
    key_send_sem,
    key_recv_sem,
    s1_send,
    s1_recv,
    s2_send,
    s2_recv,
    s3_send,
    s3_recv,
    own_send,
    col_send,
    diag_send,
    g_recv,
):
    dp_count, mp_count, values, share, capacity = dims
    outer = dp_count // 4
    total = values + share
    me = lax.axis_index("dp")
    mp = lax.axis_index("mp")
    x = me % 2
    y = (me // 2) % 2
    z = me // 4

    def place(zz, yy, xx):
        return zz * 4 + yy * 2 + xx

    x_nb = place(z, y, 1 - x)
    y_nb = place(z, 1 - y, x)
    far_first = sorted(range(1, outer), key=lambda k: -min(k, outer - k))
    order = far_first + [0]
    routes = range(capacity)

    loads = [
        pltpu.make_async_copy(value_hbm.at[0], blocks.at[pl.ds(0, values)], load_sem.at[0]),
        pltpu.make_async_copy(
            key_hbm.at[0, 0, pl.ds(mp * share, share)], key_mine, load_sem.at[1]
        ),
    ]
    for i, (src, dst) in enumerate(
        (
            (weights_hbm, weights),
            (left_hbm, left),
            (right_hbm, right),
            (lroot_hbm, lroot),
            (rroot_hbm, rroot),
            (second_hbm, second),
        )
    ):
        loads.append(pltpu.make_async_copy(src.at[0, 0], dst, load_sem.at[2 + i]))
    for copy in loads:
        copy.start()

    barrier = pltpu.get_barrier_semaphore()
    partners = [(x_nb, mp), (y_nb, mp)]
    partners += [(place((z + k) % outer, y, x), mp) for k in range(1, outer)]
    partners += [(me, (mp + k) % mp_count) for k in range(1, mp_count)]
    for partner in partners:
        pl.semaphore_signal(barrier, inc=1, device_id=partner, device_id_type=MESH)

    blocks[total] = jnp.zeros(blocks.shape[1:], blocks.dtype)

    def fill(o, carry):
        first = jnp.int32(total)
        last = jnp.int32(-1)
        for b in range(total):
            same = owners[b] == o
            first = jnp.minimum(first, jnp.where(same, b, total))
            last = jnp.maximum(last, jnp.where(same, b, -1))
        table[0, o] = first
        table[1, o] = jnp.where(last > first, last, total)
        return carry

    lax.fori_loop(0, dp_count, fill, 0)
    pl.semaphore_wait(barrier, len(partners))

    key_copies = []
    for k in range(1, mp_count):
        to = (mp + k) % mp_count
        copy = pltpu.make_async_remote_copy(
            src_ref=key_hbm.at[0, 0, pl.ds(to * share, share)],
            dst_ref=key_recv.at[k - 1],
            send_sem=key_send_sem.at[k - 1],
            recv_sem=key_recv_sem.at[k - 1],
            device_id=(me, to),
            device_id_type=MESH,
        )
        copy.start()
        key_copies.append(copy)
    loads[0].wait()
    loads[1].wait()
    for copy in key_copies:
        copy.wait_recv()
    for j in range(share):
        key_sum = key_mine[j].astype(jnp.float32)
        for k in range(1, mp_count):
            key_sum = key_sum + key_recv[k - 1, j].astype(jnp.float32)
        blocks[values + j] = key_sum.astype(blocks.dtype)

    def local(zz, yy, xx, s):
        return blocks[table[s, place(zz, yy, xx)]]

    first_copies = {}
    for c, k in enumerate(order):
        zz = (z + k) % outer
        for s in routes:
            over_x = s % 2 == 0
            for t in range(2):
                if over_x:
                    there = (zz, (1 - y) if t == 0 else y, 1 - x)
                else:
                    there = (zz, 1 - y, (1 - x) if t == 0 else x)
                send1[s, c, t] = local(*there, s)
            copy = pltpu.make_async_remote_copy(
                src_ref=send1.at[s, c],
                dst_ref=recv1.at[s, c],
                send_sem=s1_send.at[s, c],
                recv_sem=s1_recv.at[s, c],
                device_id=(x_nb if over_x else y_nb, mp),
                device_id_type=MESH,
            )
            copy.start()
            first_copies[s, c] = copy

    second_copies = {}
    third_copies = {}

    def second_step(c, k, s):
        zz = (z + k) % outer
        over_x = s % 2 == 0
        first_copies[s, c].wait_recv()
        other = (zz, 1 - y, x) if over_x else (zz, y, 1 - x)
        send2[s, c] = (
            recv1[s, c, 0].astype(jnp.float32) + local(*other, s).astype(jnp.float32)
        ).astype(send2.dtype)
        copy = pltpu.make_async_remote_copy(
            src_ref=send2.at[s, c],
            dst_ref=recv2.at[s, c],
            send_sem=s2_send.at[s, c],
            recv_sem=s2_recv.at[s, c],
            device_id=(y_nb if over_x else x_nb, mp),
            device_id_type=MESH,
        )
        copy.start()
        second_copies[s, c] = copy
        acc[s, c] = recv1[s, c, 1].astype(jnp.float32) + local(zz, y, x, s).astype(jnp.float32)

    def third_step(c, k, s):
        second_copies[s, c].wait_recv()
        part = acc[s, c] + recv2[s, c].astype(jnp.float32)
        if k == 0:
            grad[s] = part
            return
        send3[s, c] = part.astype(send3.dtype)
        copy = pltpu.make_async_remote_copy(
            src_ref=send3.at[s, c],
            dst_ref=recv3.at[s, c],
            send_sem=s3_send.at[s, c],
            recv_sem=s3_recv.at[s, c],
            device_id=(place((z + k) % outer, y, x), mp),
            device_id_type=MESH,
        )
        copy.start()
        third_copies[s, c] = copy

    for c, k in enumerate(order):
        for s in routes:
            second_step(c, k, s)
        if c > 0:
            for s in routes:
                third_step(c - 1, order[c - 1], s)
    for s in routes:
        third_step(outer - 1, 0, s)
    for copy in loads[2:]:
        copy.wait()

    for s in routes:
        gradient = grad[s]
        for c in range(outer - 1):
            third_copies[s, c].wait_recv()
            gradient = gradient + recv3[s, c].astype(jnp.float32)
        grad[s] = gradient
        product = dot(lroot[s], gradient, ((1,), (0,)))
        product = dot(product, rroot[s], ((1,), (0,)))
        new_second = ADAM_DECAY * second[s] + (1.0 - ADAM_DECAY) * gradient * gradient
        out_second[0, 0, s] = new_second
        adam_step = gradient / jnp.sqrt(new_second)
        adam_norm = jnp.sqrt(jnp.sum(adam_step * adam_step, keepdims=True))
        shaped_norm = jnp.sqrt(jnp.sum(product * product, keepdims=True))
        scale = adam_norm / (shaped_norm + NORM_EPS)
        new_weights = weights[s] - LEARN_RATE * scale * product
        out_weights[0, 0, s] = new_weights
        gathered[me, s] = new_weights.astype(gathered.dtype)

    def spread(o, s, to, send_sem, slots=1):
        part = gathered.at[o, pl.ds(s, slots)]
        copy = pltpu.make_async_remote_copy(
            src_ref=part,
            dst_ref=part,
            send_sem=send_sem,
            recv_sem=g_recv.at[o, s],
            device_id=(to, mp),
            device_id_type=MESH,
        )
        copy.start()
        return copy

    def arrived(o, s):
        part = gathered.at[o, pl.ds(s, 1)]
        pltpu.make_async_remote_copy(
            src_ref=part,
            dst_ref=part,
            send_sem=own_send.at[0, 0],
            recv_sem=g_recv.at[o, s],
            device_id=(x_nb, mp),
            device_id_type=MESH,
        ).wait_recv()

    sent = []

    def spread_plane(c, o):
        for s in routes:
            sent.append(spread(o, s, y_nb if s % 2 == 0 else x_nb, col_send.at[0, c, s]))
        for s in routes:
            sent.append(spread(o, s, x_nb if s % 2 == 0 else y_nb, col_send.at[1, c, s]))

    def spread_diagonal(c, k):
        zz = (z + k) % outer
        for s in routes:
            o = place(zz, 1 - y, x) if s % 2 == 0 else place(zz, y, 1 - x)
            arrived(o, s)
            sent.append(spread(o, s, x_nb if s % 2 == 0 else y_nb, diag_send.at[c, s]))

    for c, k in enumerate(far_first):
        for s in routes:
            sent.append(spread(me, s, place((z + k) % outer, y, x), own_send.at[c, s]))
    spread_plane(0, me)

    for s in routes:
        gradient = grad[s]
        out_left[0, 0, s] = STAT_DECAY * left[s] + (1.0 - STAT_DECAY) * dot(gradient, gradient, ((1,), (1,)))
        out_right[0, 0, s] = STAT_DECAY * right[s] + (1.0 - STAT_DECAY) * dot(
            gradient, gradient, ((0,), (0,))
        )

    near_first = far_first[::-1]
    for c, k in enumerate(near_first):
        o = place((z + outer - k) % outer, y, x)
        for s in routes:
            arrived(o, s)
        spread_plane(1 + c, o)
        if c == 0:
            spread_diagonal(0, 0)
        else:
            spread_diagonal(c, outer - near_first[c - 1])
    spread_diagonal(outer - 1, outer - near_first[-1])

    for k in [0] + [outer - k for k in near_first]:
        zz = (z + k) % outer
        for s in routes:
            arrived(place(zz, y, 1 - x) if s % 2 == 0 else place(zz, 1 - y, x), s)
            arrived(place(zz, 1 - y, 1 - x), s)

    for copy in key_copies:
        copy.wait_send()
    for copies in (first_copies, second_copies, third_copies):
        for copy in copies.values():
            copy.wait_send()
    for copy in sent:
        copy.wait_send()


def order_kernel(values, share, owners, weights, left, right, second, gathered, *rest):
    outs, (out_values, out_keys), sems = rest[:4], rest[4:6], rest[6]
    copies = []

    def go(src, dst):
        copy = pltpu.make_async_copy(src, dst, sems.at[len(copies)])
        copy.start()
        copies.append(copy)

    for src, dst in zip((weights, left, right, second), outs):
        go(src, dst)
    total = values + share
    ids = [owners[b] for b in range(total)]
    for b in range(total):
        rank = jnp.int32(0)
        for a in range(b):
            rank = rank + jnp.where(ids[a] == ids[b], 1, 0)
        dst = out_values.at[b] if b < values else out_keys.at[b - values]
        go(gathered.at[ids[b], rank], dst)
    for copy in copies:
        copy.wait()


def on_device(value_grads, key_grads, owners, weights, left, right, left_root, right_root, second):
    dp_count = lax.axis_size("dp")
    mp_count = lax.axis_size("mp")
    capacity = weights.shape[2]
    values = value_grads.shape[1]
    side = value_grads.shape[2]
    share = key_grads.shape[2] // mp_count
    total = values + share
    outer = dp_count // 4
    f32, bf16 = jnp.float32, jnp.bfloat16
    block = (side, side)
    state = jax.ShapeDtypeStruct((1, 1, capacity) + block, f32)
    owner_ids = owners[:, 0]
    hbm = pl.BlockSpec(memory_space=pl.ANY)
    smem = pl.BlockSpec(memory_space=pltpu.SMEM)
    vmem = pl.BlockSpec(memory_space=pltpu.VMEM)
    dma = pltpu.SemaphoreType.DMA
    peers = max(outer - 1, 1)
    others = max(mp_count - 1, 1)
    mid = [state] * 4 + [jax.ShapeDtypeStruct((dp_count, capacity) + block, bf16)]
    results = pl.pallas_call(
        functools.partial(main_kernel, (dp_count, mp_count, values, share, capacity)),
        out_shape=mid,
        in_specs=[smem] + [pl.BlockSpec(memory_space=pltpu.HBM)] * 8,
        out_specs=[vmem] * 5,
        scratch_shapes=[
            pltpu.SMEM((2, dp_count), jnp.int32),
            pltpu.VMEM((total + 1,) + block, bf16),
            pltpu.VMEM((share,) + block, bf16),
            pltpu.VMEM((others, share) + block, bf16),
        ]
        + [pltpu.VMEM((capacity,) + block, f32)] * 6
        + [
            pltpu.VMEM((capacity, outer, 2) + block, bf16),
            pltpu.VMEM((capacity, outer, 2) + block, bf16),
            pltpu.VMEM((capacity, outer) + block, bf16),
            pltpu.VMEM((capacity, outer) + block, bf16),
            pltpu.VMEM((capacity, outer) + block, f32),
            pltpu.VMEM((capacity, peers) + block, bf16),
            pltpu.VMEM((capacity, peers) + block, bf16),
            pltpu.VMEM((capacity,) + block, f32),
            pltpu.VMEM((capacity,) + block, f32),
            dma((8,)),
            dma((others,)),
            dma((others,)),
            dma((capacity, outer)),
            dma((capacity, outer)),
            dma((capacity, outer)),
            dma((capacity, outer)),
            dma((capacity, peers)),
            dma((capacity, peers)),
            dma((peers, capacity)),
            dma((2, outer, capacity)),
            dma((outer, capacity)),
            dma((dp_count, capacity)),
        ],
        compiler_params=pltpu.CompilerParams(
            collective_id=0, has_side_effects=True, vmem_limit_bytes=24 * 1024 * 1024
        ),
    )(
        owner_ids,
        *(
            pltpu.with_memory_space_constraint(a, pltpu.HBM)
            for a in (value_grads, key_grads, weights, left, right, left_root, right_root, second)
        ),
    )
    return pl.pallas_call(
        functools.partial(order_kernel, values, share),
        out_shape=[state] * 4
        + [jax.ShapeDtypeStruct((values,) + block, bf16), jax.ShapeDtypeStruct((share,) + block, bf16)],
        in_specs=[smem] + [hbm] * 5,
        out_specs=[hbm] * 6,
        scratch_shapes=[dma((4 + total,))],
        compiler_params=pltpu.CompilerParams(vmem_limit_bytes=8 * 1024 * 1024),
    )(owner_ids, *results)


def solution(mesh):
    state = P("dp", "mp", None, None, None)
    return jax.shard_map(
        on_device,
        mesh=mesh,
        in_specs=(P("dp", "mp", None, None), state, P("mp", None)) + (state,) * 6,
        out_specs=(state,) * 4 + (P("mp", None, None),) * 2,
        check_vma=False,
    )
```

```python
import functools

import jax
import jax.numpy as jnp
from jax import lax
from jax.experimental import pallas as pl
from jax.experimental.pallas import tpu as pltpu
from jax.sharding import PartitionSpec as P

STAT_DECAY = 0.95
ADAM_DECAY = 0.95
LEARN_RATE = 0.1
NORM_EPS = 1e-06
MESH = pl.DeviceIdType.MESH
HIGH = lax.Precision.HIGHEST


def dot(a, b, contract):
    return lax.dot_general(
        a, b, ((contract[0], contract[1]), ((), ())), precision=HIGH, preferred_element_type=jnp.float32
    )


def main_kernel(
    dims,
    owners_hbm,
    value_hbm,
    key_hbm,
    weights_hbm,
    left_hbm,
    right_hbm,
    lroot_hbm,
    rroot_hbm,
    second_hbm,
    out_weights,
    out_left,
    out_right,
    out_second,
    gathered,
    owners,
    table,
    blocks,
    key_mine,
    key_recv,
    weights,
    left,
    right,
    lroot,
    rroot,
    second,
    plane_send,
    plane_recv,
    line_send,
    line_recv,
    cross_send,
    cross_recv,
    back_send,
    back_recv,
    grad,
    load_sem,
    key_send_sem,
    key_recv_sem,
    plane_send_sem,
    plane_recv_sem,
    line_send_sem,
    line_recv_sem,
    cross_send_sem,
    cross_recv_sem,
    back_send_sem,
    back_recv_sem,
    own_send_sem,
    fan_send_sem,
    tail_fan_sem,
    tail_line_sem,
    head_recv_sem,
    tail_recv_sem,
):
    dp_count, mp_count, values, share, capacity, cut = dims
    outer = dp_count // 4
    total = values + share
    me = lax.axis_index("dp")
    mp = lax.axis_index("mp")
    x = me % 2
    y = (me // 2) % 2
    z = me // 4
    f32 = jnp.float32
    slots = range(capacity)
    head = pl.ds(0, cut)
    tail = pl.ds(cut, blocks.shape[1] - cut)

    def place(zz, yy, xx):
        return zz * 4 + yy * 2 + xx

    plane = [(1 - y, 1 - x), (y, 1 - x), (1 - y, x)]
    far_first = sorted(range(1, outer), key=lambda k: -min(k, outer - k))
    near_first = far_first[::-1]
    order = far_first + [0]

    owner_load = pltpu.make_async_copy(owners_hbm, owners, load_sem.at[8])
    owner_load.start()
    loads = [
        pltpu.make_async_copy(value_hbm.at[0], blocks.at[pl.ds(0, values)], load_sem.at[0]),
        pltpu.make_async_copy(
            key_hbm.at[0, 0, pl.ds(mp * share, share)], key_mine, load_sem.at[1]
        ),
    ]
    for i, (src, dst) in enumerate(
        (
            (weights_hbm, weights),
            (left_hbm, left),
            (right_hbm, right),
            (lroot_hbm, lroot),
            (rroot_hbm, rroot),
            (second_hbm, second),
        )
    ):
        loads.append(pltpu.make_async_copy(src.at[0, 0], dst, load_sem.at[2 + i]))
    for copy in loads:
        copy.start()

    barrier = pltpu.get_barrier_semaphore()
    partners = [(me, (mp + k) % mp_count) for k in range(1, mp_count)]
    partners += [(place(z, yy, xx), mp) for yy, xx in plane]
    partners += [(place((z + k) % outer, y, x), mp) for k in range(1, outer)]
    for partner in partners:
        pl.semaphore_signal(barrier, inc=1, device_id=partner, device_id_type=MESH)

    blocks[total] = jnp.zeros(blocks.shape[1:], blocks.dtype)
    owner_load.wait()

    def fill(o, carry):
        first = jnp.int32(total)
        last = jnp.int32(-1)
        for b in range(total):
            same = owners[b] == o
            first = jnp.minimum(first, jnp.where(same, b, total))
            last = jnp.maximum(last, jnp.where(same, b, -1))
        table[0, o] = first
        table[1, o] = jnp.where(last > first, last, total)
        return carry

    lax.fori_loop(0, dp_count, fill, 0)
    pl.semaphore_wait(barrier, len(partners))

    sent = []

    def remote(src, dst, send_sem, recv_sem, to):
        copy = pltpu.make_async_remote_copy(
            src_ref=src,
            dst_ref=dst,
            send_sem=send_sem,
            recv_sem=recv_sem,
            device_id=to,
            device_id_type=MESH,
        )
        copy.start()
        sent.append(copy)
        return copy

    key_copies = []
    for k in range(1, mp_count):
        to = (mp + k) % mp_count
        key_copies.append(
            remote(
                key_hbm.at[0, 0, pl.ds(to * share, share)],
                key_recv.at[k - 1],
                key_send_sem.at[k - 1],
                key_recv_sem.at[k - 1],
                (me, to),
            )
        )
    loads[0].wait()
    loads[1].wait()
    for copy in key_copies:
        copy.wait_recv()
    for j in range(share):
        key_sum = key_mine[j].astype(f32)
        for k in range(1, mp_count):
            key_sum = key_sum + key_recv[k - 1, j].astype(f32)
        blocks[values + j] = key_sum.astype(blocks.dtype)

    plane_copies, cross_copies = {}, {}

    def start_plane(c):
        zz = (z + order[c]) % outer
        for q, (yy, xx) in enumerate(plane):
            for s in slots:
                plane_send[c, q, s] = blocks[table[s, place(zz, yy, xx)], head]
            plane_copies[c, q] = remote(
                plane_send.at[c, q],
                plane_recv.at[c, q],
                plane_send_sem.at[c, q],
                plane_recv_sem.at[c, q],
                (place(z, yy, xx), mp),
            )

    def start_cross(c):
        zz = (z + order[c]) % outer
        for q in range(4):
            for s in slots:
                cross_send[c, q, s] = blocks[table[s, zz * 4 + q], tail]
        cross_copies[c] = remote(
            cross_send.at[c],
            cross_recv.at[c],
            cross_send_sem.at[c],
            cross_recv_sem.at[c],
            (place(zz, y, x), mp),
        )

    for c in range(outer):
        start_plane(c)
        if c < outer - 1:
            start_cross(c)

    line_copies, back_copies = {}, {}

    def plane_sum(c, s):
        part = blocks[table[s, place((z + order[c]) % outer, y, x)], head].astype(f32)
        for q in range(3):
            part = part + plane_recv[c, q, s].astype(f32)
        return part

    def start_line(c):
        for q in range(3):
            plane_copies[c, q].wait_recv()
        for s in slots:
            line_send[c, s] = plane_sum(c, s).astype(line_send.dtype)
        line_copies[c] = remote(
            line_send.at[c],
            line_recv.at[c],
            line_send_sem.at[c],
            line_recv_sem.at[c],
            (place((z + order[c]) % outer, y, x), mp),
        )

    def cross_sum(yy, xx, s):
        part = blocks[table[s, place(z, yy, xx)], tail].astype(f32)
        for c in range(outer - 1):
            part = part + cross_recv[c, yy * 2 + xx, s].astype(f32)
        return part

    def start_back():
        for c in range(outer - 1):
            cross_copies[c].wait_recv()
        for q, (yy, xx) in enumerate(plane):
            for s in slots:
                back_send[q, s] = cross_sum(yy, xx, s).astype(back_send.dtype)
            back_copies[q] = remote(
                back_send.at[q],
                back_recv.at[q],
                back_send_sem.at[q],
                back_recv_sem.at[q],
                (place(z, yy, xx), mp),
            )

    half = outer // 2
    for c in range(half):
        start_line(c)
    start_back()
    for c in range(half, outer - 1):
        start_line(c)
    for q in range(3):
        plane_copies[outer - 1, q].wait_recv()
    for s in slots:
        grad[s, head] = plane_sum(outer - 1, s)
        grad[s, tail] = cross_sum(y, x, s)
    for q in range(3):
        back_copies[q].wait_recv()
    for s in slots:
        part = grad[s, tail]
        for q in range(3):
            part = part + back_recv[q, s].astype(f32)
        grad[s, tail] = part
    for c in range(outer - 1):
        line_copies[c].wait_recv()
    for s in slots:
        part = grad[s, head]
        for c in range(outer - 1):
            part = part + line_recv[c, s].astype(f32)
        grad[s, head] = part
    for copy in loads[2:]:
        copy.wait()

    for s in slots:
        gradient = grad[s]
        shaped = dot(lroot[s], gradient, ((1,), (0,)))
        shaped = dot(shaped, rroot[s], ((1,), (0,)))
        new_second = ADAM_DECAY * second[s] + (1.0 - ADAM_DECAY) * gradient * gradient
        out_second[0, 0, s] = new_second
        adam_step = gradient / jnp.sqrt(new_second)
        adam_norm = jnp.sqrt(jnp.sum(adam_step * adam_step, keepdims=True))
        shaped_norm = jnp.sqrt(jnp.sum(shaped * shaped, keepdims=True))
        scale = adam_norm / (shaped_norm + NORM_EPS)
        new_weights = weights[s] - LEARN_RATE * scale * shaped
        out_weights[0, 0, s] = new_weights
        gathered[me, s] = new_weights.astype(gathered.dtype)

    def heads(o):
        return gathered.at[o, :, head]

    def tails(o, count=1):
        return gathered.at[pl.ds(o, count), :, tail]

    def await_heads(o):
        pltpu.make_async_remote_copy(
            src_ref=heads(o),
            dst_ref=heads(o),
            send_sem=own_send_sem.at[0],
            recv_sem=head_recv_sem.at[o],
            device_id=(place(z, y, 1 - x), mp),
            device_id_type=MESH,
        ).wait_recv()

    def await_tails(o, count, sem):
        pltpu.make_async_remote_copy(
            src_ref=tails(o, count),
            dst_ref=tails(o, count),
            send_sem=own_send_sem.at[0],
            recv_sem=tail_recv_sem.at[sem],
            device_id=(place(z, y, 1 - x), mp),
            device_id_type=MESH,
        ).wait_recv()

    def fan_heads(c, o):
        for q, (yy, xx) in enumerate(plane):
            remote(
                heads(o), heads(o), fan_send_sem.at[c, q], head_recv_sem.at[o], (place(z, yy, xx), mp)
            )

    for c, k in enumerate(near_first):
        remote(
            heads(me),
            heads(me),
            own_send_sem.at[c],
            head_recv_sem.at[me],
            (place((z + k) % outer, y, x), mp),
        )
    for q, (yy, xx) in enumerate(plane):
        remote(
            tails(me), tails(me), tail_fan_sem.at[q], tail_recv_sem.at[q], (place(z, yy, xx), mp)
        )
    fan_heads(0, me)

    def stats(s):
        gradient = grad[s]
        out_left[0, 0, s] = STAT_DECAY * left[s] + (1.0 - STAT_DECAY) * dot(gradient, gradient, ((1,), (1,)))
        out_right[0, 0, s] = STAT_DECAY * right[s] + (1.0 - STAT_DECAY) * dot(
            gradient, gradient, ((0,), (0,))
        )

    for s in slots:
        stats(s)

    for q, (yy, xx) in enumerate(plane):
        await_tails(place(z, yy, xx), 1, q)
    for c, k in enumerate(near_first):
        remote(
            tails(z * 4, 4),
            tails(z * 4, 4),
            tail_line_sem.at[c],
            tail_recv_sem.at[2 + k],
            (place((z + k) % outer, y, x), mp),
        )
    for c, k in enumerate(near_first):
        o = place((z + outer - k) % outer, y, x)
        await_heads(o)
        fan_heads(1 + c, o)
    for k in [0] + near_first:
        for yy, xx in plane:
            await_heads(place((z + outer - k) % outer, yy, xx))
    for k in near_first:
        await_tails((z + outer - k) % outer * 4, 4, 2 + k)

    for copy in sent:
        copy.wait_send()


def order_kernel(values, share, owners_hbm, weights, left, right, second, gathered, *rest):
    outs, (out_values, out_keys), owners, sems, owner_sem = rest[:4], rest[4:6], rest[6], rest[7], rest[8]
    copies = []
    owner_load = pltpu.make_async_copy(owners_hbm, owners, owner_sem)
    owner_load.start()

    def go(src, dst):
        copy = pltpu.make_async_copy(src, dst, sems.at[len(copies)])
        copy.start()
        copies.append(copy)

    for src, dst in zip((weights, left, right, second), outs):
        go(src, dst)
    total = values + share
    owner_load.wait()
    ids = [owners[b] for b in range(total)]
    for b in range(total):
        rank = jnp.int32(0)
        for a in range(b):
            rank = rank + jnp.where(ids[a] == ids[b], 1, 0)
        dst = out_values.at[b] if b < values else out_keys.at[b - values]
        go(gathered.at[ids[b], rank], dst)
    for copy in copies:
        copy.wait()


def on_device(value_grads, key_grads, owners, weights, left, right, left_root, right_root, second):
    dp_count = lax.axis_size("dp")
    mp_count = lax.axis_size("mp")
    capacity = weights.shape[2]
    values = value_grads.shape[1]
    side = value_grads.shape[2]
    share = key_grads.shape[2] // mp_count
    total = values + share
    outer = dp_count // 4
    f32, bf16 = jnp.float32, jnp.bfloat16
    block = (side, side)
    state = jax.ShapeDtypeStruct((1, 1, capacity) + block, f32)
    owner_ids = pltpu.with_memory_space_constraint(owners[:, 0], pltpu.HBM)
    hbm = pl.BlockSpec(memory_space=pl.ANY)
    vmem = pl.BlockSpec(memory_space=pltpu.VMEM)
    dma = pltpu.SemaphoreType.DMA
    peers = max(outer - 1, 1)
    others = max(mp_count - 1, 1)
    cut = side - side // 4
    head, tail = (cut, side), (side - cut, side)
    mid = [state] * 4 + [jax.ShapeDtypeStruct((dp_count, capacity) + block, bf16)]
    results = pl.pallas_call(
        functools.partial(main_kernel, (dp_count, mp_count, values, share, capacity, cut)),
        out_shape=mid,
        in_specs=[hbm] * 9,
        out_specs=[vmem] * 5,
        scratch_shapes=[
            pltpu.SMEM((total,), jnp.int32),
            pltpu.SMEM((2, dp_count), jnp.int32),
            pltpu.VMEM((total + 1,) + block, bf16),
            pltpu.VMEM((share,) + block, bf16),
            pltpu.VMEM((others, share) + block, bf16),
        ]
        + [pltpu.VMEM((capacity,) + block, f32)] * 6
        + [pltpu.VMEM((outer, 3, capacity) + head, bf16)] * 2
        + [pltpu.VMEM((peers, capacity) + head, bf16)] * 2
        + [pltpu.VMEM((peers, 4, capacity) + tail, bf16)] * 2
        + [pltpu.VMEM((3, capacity) + tail, bf16)] * 2
        + [pltpu.VMEM((capacity,) + block, f32)]
        + [dma((9,)), dma((others,)), dma((others,))]
        + [dma((outer, 3))] * 2
        + [dma((peers,))] * 4
        + [dma((3,))] * 2
        + [dma((peers,)), dma((outer, 3)), dma((3,)), dma((peers,)), dma((dp_count,)), dma((3 + peers,))],
        compiler_params=pltpu.CompilerParams(
            collective_id=0, has_side_effects=True, vmem_limit_bytes=32 * 1024 * 1024
        ),
    )(
        owner_ids,
        *(
            pltpu.with_memory_space_constraint(a, pltpu.HBM)
            for a in (value_grads, key_grads, weights, left, right, left_root, right_root, second)
        ),
    )
    return pl.pallas_call(
        functools.partial(order_kernel, values, share),
        out_shape=[state] * 4
        + [jax.ShapeDtypeStruct((values,) + block, bf16), jax.ShapeDtypeStruct((share,) + block, bf16)],
        in_specs=[hbm] * 6,
        out_specs=[hbm] * 6,
        scratch_shapes=[pltpu.SMEM((total,), jnp.int32), dma((4 + total,)), dma],
        compiler_params=pltpu.CompilerParams(vmem_limit_bytes=8 * 1024 * 1024),
    )(owner_ids, *results)


def solution(mesh):
    state = P("dp", "mp", None, None, None)
    return jax.shard_map(
        on_device,
        mesh=mesh,
        in_specs=(P("dp", "mp", None, None), state, P("mp", None)) + (state,) * 6,
        out_specs=(state,) * 4 + (P("mp", None, None),) * 2,
        check_vma=False,
    )
```

```python
import functools

import jax
import jax.numpy as jnp
from jax import lax
from jax.experimental import pallas as pl
from jax.experimental.pallas import tpu as pltpu
from jax.sharding import PartitionSpec as P

STAT_DECAY = 0.95
ADAM_DECAY = 0.95
LEARN_RATE = 0.1
NORM_EPS = 1e-06
MESH = pl.DeviceIdType.MESH
HIGH = lax.Precision.HIGHEST


def dot(a, b, contract):
    return lax.dot_general(
        a, b, ((contract[0], contract[1]), ((), ())), precision=HIGH, preferred_element_type=jnp.float32
    )


def main_kernel(
    dims,
    owners_hbm,
    value_hbm,
    key_hbm,
    weights_hbm,
    left_hbm,
    right_hbm,
    lroot_hbm,
    rroot_hbm,
    second_hbm,
    out_weights,
    out_left,
    out_right,
    out_second,
    out_values,
    out_keys,
    gathered,
    owners,
    table,
    blocks,
    key_mine,
    key_recv,
    weights,
    left,
    right,
    lroot,
    rroot,
    second,
    plane_send,
    plane_recv,
    line_send,
    line_recv,
    cross_send,
    cross_recv,
    back_send,
    back_recv,
    grad,
    load_sem,
    key_send_sem,
    key_recv_sem,
    plane_send_sem,
    plane_recv_sem,
    line_send_sem,
    line_recv_sem,
    cross_send_sem,
    cross_recv_sem,
    back_send_sem,
    back_recv_sem,
    own_send_sem,
    fan_send_sem,
    tail_fan_sem,
    tail_line_sem,
    head_recv_sem,
    tail_recv_sem,
):
    dp_count, mp_count, values, share, capacity, cut = dims
    outer = dp_count // 4
    total = values + share
    me = lax.axis_index("dp")
    mp = lax.axis_index("mp")
    x = me % 2
    y = (me // 2) % 2
    z = me // 4
    f32 = jnp.float32
    slots = range(capacity)
    head = pl.ds(0, cut)
    tail = pl.ds(cut, blocks.shape[1] - cut)

    def place(zz, yy, xx):
        return zz * 4 + yy * 2 + xx

    plane = [(1 - y, 1 - x), (y, 1 - x), (1 - y, x)]
    far_first = sorted(range(1, outer), key=lambda k: -min(k, outer - k))
    near_first = far_first[::-1]
    order = far_first + [0]

    owner_load = pltpu.make_async_copy(owners_hbm, owners, load_sem.at[8])
    owner_load.start()
    loads = [
        pltpu.make_async_copy(value_hbm.at[0], blocks.at[pl.ds(0, values)], load_sem.at[0]),
        pltpu.make_async_copy(
            key_hbm.at[0, 0, pl.ds(mp * share, share)], key_mine, load_sem.at[1]
        ),
    ]
    for i, (src, dst) in enumerate(
        (
            (weights_hbm, weights),
            (left_hbm, left),
            (right_hbm, right),
            (lroot_hbm, lroot),
            (rroot_hbm, rroot),
            (second_hbm, second),
        )
    ):
        loads.append(pltpu.make_async_copy(src.at[0, 0], dst, load_sem.at[2 + i]))
    for copy in loads[:2]:
        copy.start()
    sent = []

    barrier = pltpu.get_barrier_semaphore()
    partners = [(me, (mp + k) % mp_count) for k in range(1, mp_count)]
    partners += [(place(z, yy, xx), mp) for yy, xx in plane]
    partners += [(place((z + k) % outer, y, x), mp) for k in range(1, outer)]
    for partner in partners:
        pl.semaphore_signal(barrier, inc=1, device_id=partner, device_id_type=MESH)

    def remote(src, dst, send_sem, recv_sem, to):
        copy = pltpu.make_async_remote_copy(
            src_ref=src,
            dst_ref=dst,
            send_sem=send_sem,
            recv_sem=recv_sem,
            device_id=to,
            device_id_type=MESH,
        )
        copy.start()
        sent.append(copy)
        return copy

    pl.semaphore_wait(barrier, len(partners))

    key_copies = []
    for k in range(1, mp_count):
        to = (mp + k) % mp_count
        key_copies.append(
            remote(
                key_hbm.at[0, 0, pl.ds(to * share, share)],
                key_recv.at[k - 1],
                key_send_sem.at[k - 1],
                key_recv_sem.at[k - 1],
                (me, to),
            )
        )

    blocks[total] = jnp.zeros(blocks.shape[1:], blocks.dtype)
    owner_load.wait()

    def fill(o, carry):
        first = jnp.int32(total)
        last = jnp.int32(-1)
        for b in range(total):
            same = owners[b] == o
            first = jnp.minimum(first, jnp.where(same, b, total))
            last = jnp.maximum(last, jnp.where(same, b, -1))
        table[0, o] = first
        table[1, o] = jnp.where(last > first, last, total)
        return carry

    lax.fori_loop(0, dp_count, fill, 0)
    loads[0].wait()
    loads[1].wait()
    for copy in key_copies:
        copy.wait_recv()
    for j in range(share):
        key_sum = key_mine[j].astype(f32)
        for k in range(1, mp_count):
            key_sum = key_sum + key_recv[k - 1, j].astype(f32)
        blocks[values + j] = key_sum.astype(blocks.dtype)

    plane_copies, cross_copies = {}, {}

    def start_plane(c):
        zz = (z + order[c]) % outer
        for q, (yy, xx) in enumerate(plane):
            for s in slots:
                plane_send[c, q, s] = blocks[table[s, place(zz, yy, xx)], head]
            plane_copies[c, q] = remote(
                plane_send.at[c, q],
                plane_recv.at[c, q],
                plane_send_sem.at[c, q],
                plane_recv_sem.at[c, q],
                (place(z, yy, xx), mp),
            )

    def start_cross(c):
        zz = (z + order[c]) % outer
        for q in range(4):
            for s in slots:
                cross_send[c, q, s] = blocks[table[s, zz * 4 + q], tail]
        cross_copies[c] = remote(
            cross_send.at[c],
            cross_recv.at[c],
            cross_send_sem.at[c],
            cross_recv_sem.at[c],
            (place(zz, y, x), mp),
        )

    for c in range(outer):
        start_plane(c)
        if c < outer - 1:
            start_cross(c)
    for copy in loads[2:]:
        copy.start()

    line_copies, back_copies = {}, {}

    def plane_sum(c, s):
        part = blocks[table[s, place((z + order[c]) % outer, y, x)], head].astype(f32)
        for q in range(3):
            part = part + plane_recv[c, q, s].astype(f32)
        return part

    def start_line(c):
        for q in range(3):
            plane_copies[c, q].wait_recv()
        for s in slots:
            line_send[c, s] = plane_sum(c, s).astype(line_send.dtype)
        line_copies[c] = remote(
            line_send.at[c],
            line_recv.at[c],
            line_send_sem.at[c],
            line_recv_sem.at[c],
            (place((z + order[c]) % outer, y, x), mp),
        )

    def cross_sum(yy, xx, s):
        part = blocks[table[s, place(z, yy, xx)], tail].astype(f32)
        for c in range(outer - 1):
            part = part + cross_recv[c, yy * 2 + xx, s].astype(f32)
        return part

    def start_back():
        for c in range(outer - 1):
            cross_copies[c].wait_recv()
        for q, (yy, xx) in enumerate(plane):
            for s in slots:
                back_send[q, s] = cross_sum(yy, xx, s).astype(back_send.dtype)
            back_copies[q] = remote(
                back_send.at[q],
                back_recv.at[q],
                back_send_sem.at[q],
                back_recv_sem.at[q],
                (place(z, yy, xx), mp),
            )

    half = outer // 2
    for c in range(half):
        start_line(c)
    start_back()
    for c in range(half, outer - 1):
        start_line(c)
    for q in range(3):
        plane_copies[outer - 1, q].wait_recv()
    for s in slots:
        grad[s, head] = plane_sum(outer - 1, s)
        grad[s, tail] = cross_sum(y, x, s)
    for q in range(3):
        back_copies[q].wait_recv()
    for s in slots:
        part = grad[s, tail]
        for q in range(3):
            part = part + back_recv[q, s].astype(f32)
        grad[s, tail] = part
    for c in range(outer - 1):
        line_copies[c].wait_recv()
    for s in slots:
        part = grad[s, head]
        for c in range(outer - 1):
            part = part + line_recv[c, s].astype(f32)
        grad[s, head] = part
    for copy in loads[2:]:
        copy.wait()

    for s in slots:
        gradient = grad[s]
        shaped = dot(lroot[s], gradient, ((1,), (0,)))
        shaped = dot(shaped, rroot[s], ((1,), (0,)))
        new_second = ADAM_DECAY * second[s] + (1.0 - ADAM_DECAY) * gradient * gradient
        out_second[0, 0, s] = new_second
        adam_step = gradient / jnp.sqrt(new_second)
        adam_norm = jnp.sqrt(jnp.sum(adam_step * adam_step, keepdims=True))
        shaped_norm = jnp.sqrt(jnp.sum(shaped * shaped, keepdims=True))
        scale = adam_norm / (shaped_norm + NORM_EPS)
        new_weights = weights[s] - LEARN_RATE * scale * shaped
        out_weights[0, 0, s] = new_weights
        gathered[me, s] = new_weights.astype(gathered.dtype)

    def heads(o):
        return gathered.at[o, :, head]

    def tails(o, count=1):
        return gathered.at[pl.ds(o, count), :, tail]

    def await_heads(o):
        pltpu.make_async_remote_copy(
            src_ref=heads(o),
            dst_ref=heads(o),
            send_sem=own_send_sem.at[0],
            recv_sem=head_recv_sem.at[o],
            device_id=(place(z, y, 1 - x), mp),
            device_id_type=MESH,
        ).wait_recv()

    def await_tails(o, count, sem):
        pltpu.make_async_remote_copy(
            src_ref=tails(o, count),
            dst_ref=tails(o, count),
            send_sem=own_send_sem.at[0],
            recv_sem=tail_recv_sem.at[sem],
            device_id=(place(z, y, 1 - x), mp),
            device_id_type=MESH,
        ).wait_recv()

    def fan_heads(c, o):
        for q, (yy, xx) in enumerate(plane):
            remote(
                heads(o), heads(o), fan_send_sem.at[c, q], head_recv_sem.at[o], (place(z, yy, xx), mp)
            )

    for c, k in enumerate(near_first):
        remote(
            heads(me),
            heads(me),
            own_send_sem.at[c],
            head_recv_sem.at[me],
            (place((z + k) % outer, y, x), mp),
        )
    for q, (yy, xx) in enumerate(plane):
        remote(
            tails(me), tails(me), tail_fan_sem.at[q], tail_recv_sem.at[q], (place(z, yy, xx), mp)
        )
    fan_heads(0, me)

    def stats(s):
        gradient = grad[s]
        out_left[0, 0, s] = STAT_DECAY * left[s] + (1.0 - STAT_DECAY) * dot(gradient, gradient, ((1,), (1,)))
        out_right[0, 0, s] = STAT_DECAY * right[s] + (1.0 - STAT_DECAY) * dot(
            gradient, gradient, ((0,), (0,))
        )

    for s in slots:
        stats(s)

    for q, (yy, xx) in enumerate(plane):
        await_tails(place(z, yy, xx), 1, q)
    for c, k in enumerate(near_first):
        remote(
            tails(z * 4, 4),
            tails(z * 4, 4),
            tail_line_sem.at[c],
            tail_recv_sem.at[2 + k],
            (place((z + k) % outer, y, x), mp),
        )
    for c, k in enumerate(near_first):
        o = place((z + outer - k) % outer, y, x)
        await_heads(o)
        fan_heads(1 + c, o)
    for k in [0] + near_first:
        for yy, xx in plane:
            await_heads(place((z + outer - k) % outer, yy, xx))
    for k in near_first:
        await_tails((z + outer - k) % outer * 4, 4, 2 + k)

    for b in range(total):
        owner = owners[b]
        block = gathered[owner, jnp.where(table[0, owner] == b, 0, 1)]
        if b < values:
            out_values[b] = block
        else:
            out_keys[b - values] = block
    for copy in sent:
        copy.wait_send()


def store_kernel(*refs):
    half = (len(refs) - 1) // 2
    copies = [
        pltpu.make_async_copy(src, dst, refs[-1].at[i])
        for i, (src, dst) in enumerate(zip(refs[:half], refs[half:-1]))
    ]
    for copy in copies:
        copy.start()
    for copy in copies:
        copy.wait()


def on_device(value_grads, key_grads, owners, weights, left, right, left_root, right_root, second):
    dp_count = lax.axis_size("dp")
    mp_count = lax.axis_size("mp")
    capacity = weights.shape[2]
    values = value_grads.shape[1]
    side = value_grads.shape[2]
    share = key_grads.shape[2] // mp_count
    total = values + share
    outer = dp_count // 4
    f32, bf16 = jnp.float32, jnp.bfloat16
    block = (side, side)
    state = jax.ShapeDtypeStruct((1, 1, capacity) + block, f32)
    owner_ids = pltpu.with_memory_space_constraint(owners[:, 0], pltpu.HBM)
    hbm = pl.BlockSpec(memory_space=pl.ANY)
    vmem = pl.BlockSpec(memory_space=pltpu.VMEM)
    dma = pltpu.SemaphoreType.DMA
    peers = max(outer - 1, 1)
    others = max(mp_count - 1, 1)
    cut = side - side // 4
    head, tail = (cut, side), (side - cut, side)
    results_shape = [state] * 4 + [
        jax.ShapeDtypeStruct((values,) + block, bf16),
        jax.ShapeDtypeStruct((share,) + block, bf16),
    ]
    results = pl.pallas_call(
        functools.partial(main_kernel, (dp_count, mp_count, values, share, capacity, cut)),
        out_shape=results_shape,
        in_specs=[hbm] * 9,
        out_specs=[vmem] * 6,
        scratch_shapes=[
            pltpu.VMEM((dp_count, capacity) + block, bf16),
            pltpu.SMEM((total,), jnp.int32),
            pltpu.SMEM((2, dp_count), jnp.int32),
            pltpu.VMEM((total + 1,) + block, bf16),
            pltpu.VMEM((share,) + block, bf16),
            pltpu.VMEM((others, share) + block, bf16),
        ]
        + [pltpu.VMEM((capacity,) + block, f32)] * 6
        + [pltpu.VMEM((outer, 3, capacity) + head, bf16)] * 2
        + [pltpu.VMEM((peers, capacity) + head, bf16)] * 2
        + [pltpu.VMEM((peers, 4, capacity) + tail, bf16)] * 2
        + [pltpu.VMEM((3, capacity) + tail, bf16)] * 2
        + [pltpu.VMEM((capacity,) + block, f32)]
        + [dma((9,)), dma((others,)), dma((others,))]
        + [dma((outer, 3))] * 2
        + [dma((peers,))] * 4
        + [dma((3,))] * 2
        + [dma((peers,)), dma((outer, 3)), dma((3,)), dma((peers,)), dma((dp_count,)), dma((3 + peers,))],
        compiler_params=pltpu.CompilerParams(
            collective_id=0, has_side_effects=True, vmem_limit_bytes=32 * 1024 * 1024
        ),
    )(
        owner_ids,
        *(
            pltpu.with_memory_space_constraint(a, pltpu.HBM)
            for a in (value_grads, key_grads, weights, left, right, left_root, right_root, second)
        ),
    )
    return pl.pallas_call(
        store_kernel,
        out_shape=results_shape,
        in_specs=[hbm] * 6,
        out_specs=[hbm] * 6,
        scratch_shapes=[dma((6,))],
        compiler_params=pltpu.CompilerParams(vmem_limit_bytes=8 * 1024 * 1024),
    )(*results)


def solution(mesh):
    state = P("dp", "mp", None, None, None)
    return jax.shard_map(
        on_device,
        mesh=mesh,
        in_specs=(P("dp", "mp", None, None), state, P("mp", None)) + (state,) * 6,
        out_specs=(state,) * 4 + (P("mp", None, None),) * 2,
        check_vma=False,
    )
```

```python
import functools

import jax
import jax.numpy as jnp
from jax import lax
from jax.experimental import pallas as pl
from jax.experimental.pallas import tpu as pltpu
from jax.sharding import PartitionSpec as P

STAT_DECAY = 0.95
ADAM_DECAY = 0.95
LEARN_RATE = 0.1
NORM_EPS = 1e-06
MESH = pl.DeviceIdType.MESH
HIGH = lax.Precision.HIGHEST


def dot(a, b, contract):
    return lax.dot_general(
        a, b, ((contract[0], contract[1]), ((), ())), precision=HIGH, preferred_element_type=jnp.float32
    )


def main_kernel(
    dims,
    owners_hbm,
    value_hbm,
    key_hbm,
    weights_hbm,
    left_hbm,
    right_hbm,
    lroot_hbm,
    rroot_hbm,
    second_hbm,
    out_weights,
    out_left,
    out_right,
    out_second,
    out_values,
    out_keys,
    gathered,
    owners,
    table,
    blocks,
    key_mine,
    key_recv,
    weights,
    left,
    right,
    lroot,
    rroot,
    second,
    plane_send,
    plane_recv,
    line_send,
    line_recv,
    cross_send,
    cross_recv,
    back_send,
    back_recv,
    grad,
    load_sem,
    key_send_sem,
    key_recv_sem,
    plane_send_sem,
    plane_recv_sem,
    line_send_sem,
    line_recv_sem,
    cross_send_sem,
    cross_recv_sem,
    back_send_sem,
    back_recv_sem,
    own_send_sem,
    fan_send_sem,
    tail_fan_sem,
    tail_line_sem,
    head_recv_sem,
    plane_tail_sem,
    line_tail_sem,
    relay_sem,
    turn_sem,
):
    dp_count, mp_count, values, share, capacity, cut, out_cut = dims
    outer = dp_count // 4
    total = values + share
    me = lax.axis_index("dp")
    mp = lax.axis_index("mp")
    x = me % 2
    y = (me // 2) % 2
    z = me // 4
    f32 = jnp.float32
    slots = range(capacity)
    head = pl.ds(0, cut)
    tail = pl.ds(cut, blocks.shape[1] - cut)

    def place(zz, yy, xx):
        return zz * 4 + yy * 2 + xx

    plane = [(1 - y, 1 - x), (y, 1 - x), (1 - y, x)]
    far_first = sorted(range(1, outer), key=lambda k: -min(k, outer - k))
    order = far_first + [0]

    owner_load = pltpu.make_async_copy(owners_hbm, owners, load_sem.at[8])
    owner_load.start()
    loads = [
        pltpu.make_async_copy(value_hbm.at[0], blocks.at[pl.ds(0, values)], load_sem.at[0]),
        pltpu.make_async_copy(
            key_hbm.at[0, 0, pl.ds(mp * share, share)], key_mine, load_sem.at[1]
        ),
    ]
    for i, (src, dst) in enumerate(
        (
            (weights_hbm, weights),
            (left_hbm, left),
            (right_hbm, right),
            (lroot_hbm, lroot),
            (rroot_hbm, rroot),
            (second_hbm, second),
        )
    ):
        loads.append(pltpu.make_async_copy(src.at[0, 0], dst, load_sem.at[2 + i]))
    for copy in loads[:2]:
        copy.start()
    sent = []

    barrier = pltpu.get_barrier_semaphore()
    partners = [(me, (mp + k) % mp_count) for k in range(1, mp_count)]
    partners += [(place(z, yy, xx), mp) for yy, xx in plane]
    partners += [(place((z + k) % outer, y, x), mp) for k in range(1, outer)]
    for partner in partners:
        pl.semaphore_signal(barrier, inc=1, device_id=partner, device_id_type=MESH)

    def remote(src, dst, send_sem, recv_sem, to):
        copy = pltpu.make_async_remote_copy(
            src_ref=src,
            dst_ref=dst,
            send_sem=send_sem,
            recv_sem=recv_sem,
            device_id=to,
            device_id_type=MESH,
        )
        copy.start()
        sent.append(copy)
        return copy

    pl.semaphore_wait(barrier, len(partners))

    key_copies = []
    for k in range(1, mp_count):
        to = (mp + k) % mp_count
        key_copies.append(
            remote(
                key_hbm.at[0, 0, pl.ds(to * share, share)],
                key_recv.at[k - 1],
                key_send_sem.at[k - 1],
                key_recv_sem.at[k - 1],
                (me, to),
            )
        )

    blocks[total] = jnp.zeros(blocks.shape[1:], blocks.dtype)
    owner_load.wait()

    def fill(o, carry):
        first = jnp.int32(total)
        last = jnp.int32(-1)
        for b in range(total):
            same = owners[b] == o
            first = jnp.minimum(first, jnp.where(same, b, total))
            last = jnp.maximum(last, jnp.where(same, b, -1))
        table[0, o] = first
        table[1, o] = jnp.where(last > first, last, total)
        return carry

    lax.fori_loop(0, dp_count, fill, 0)
    loads[0].wait()
    loads[1].wait()
    for copy in key_copies:
        copy.wait_recv()
    for j in range(share):
        key_sum = key_mine[j].astype(f32)
        for k in range(1, mp_count):
            key_sum = key_sum + key_recv[k - 1, j].astype(f32)
        blocks[values + j] = key_sum.astype(blocks.dtype)

    plane_copies, cross_copies = {}, {}

    def start_plane(c):
        zz = (z + order[c]) % outer
        for q, (yy, xx) in enumerate(plane):
            for s in slots:
                plane_send[c, q, s] = blocks[table[s, place(zz, yy, xx)], head]
            plane_copies[c, q] = remote(
                plane_send.at[c, q],
                plane_recv.at[c, q],
                plane_send_sem.at[c, q],
                plane_recv_sem.at[c, q],
                (place(z, yy, xx), mp),
            )

    def start_cross(c):
        zz = (z + order[c]) % outer
        for q in range(4):
            for s in slots:
                cross_send[c, q, s] = blocks[table[s, zz * 4 + q], tail]
        cross_copies[c] = remote(
            cross_send.at[c],
            cross_recv.at[c],
            cross_send_sem.at[c],
            cross_recv_sem.at[c],
            (place(zz, y, x), mp),
        )

    if mp_count % 2 == 0:

        @pl.when(mp % 2 == 1)
        def _():
            pl.semaphore_wait(turn_sem, 1)

    for c in range(outer):
        start_plane(c)
        if c < outer - 1:
            start_cross(c)
    for copy in loads[2:]:
        copy.start()

    line_copies, back_copies = {}, {}

    def plane_sum(c, s):
        part = blocks[table[s, place((z + order[c]) % outer, y, x)], head].astype(f32)
        for q in range(3):
            part = part + plane_recv[c, q, s].astype(f32)
        return part

    def start_line(c):
        for q in range(3):
            plane_copies[c, q].wait_recv()
        for s in slots:
            line_send[c, s] = plane_sum(c, s).astype(line_send.dtype)
        line_copies[c] = remote(
            line_send.at[c],
            line_recv.at[c],
            line_send_sem.at[c],
            line_recv_sem.at[c],
            (place((z + order[c]) % outer, y, x), mp),
        )

    def cross_sum(yy, xx, s):
        part = blocks[table[s, place(z, yy, xx)], tail].astype(f32)
        for c in range(outer - 1):
            part = part + cross_recv[c, yy * 2 + xx, s].astype(f32)
        return part

    def start_back():
        for c in range(outer - 1):
            cross_copies[c].wait_recv()
        for q, (yy, xx) in enumerate(plane):
            for s in slots:
                back_send[q, s] = cross_sum(yy, xx, s).astype(back_send.dtype)
            back_copies[q] = remote(
                back_send.at[q],
                back_recv.at[q],
                back_send_sem.at[q],
                back_recv_sem.at[q],
                (place(z, yy, xx), mp),
            )

    half = outer // 2
    for c in range(half):
        start_line(c)
        if c == 0:
            if mp_count % 2 == 0:

                @pl.when(mp % 2 == 0)
                def _():
                    pl.semaphore_signal(turn_sem, inc=1, device_id=(me, mp + 1), device_id_type=MESH)
    start_back()
    for c in range(half, outer - 1):
        start_line(c)
    for q in range(3):
        plane_copies[outer - 1, q].wait_recv()
    for s in slots:
        grad[s, head] = plane_sum(outer - 1, s)
        grad[s, tail] = cross_sum(y, x, s)
    for q in range(3):
        back_copies[q].wait_recv()
    for s in slots:
        part = grad[s, tail]
        for q in range(3):
            part = part + back_recv[q, s].astype(f32)
        grad[s, tail] = part
    for c in range(outer - 1):
        line_copies[c].wait_recv()
    for s in slots:
        part = grad[s, head]
        for c in range(outer - 1):
            part = part + line_recv[c, s].astype(f32)
        grad[s, head] = part
    for copy in loads[2:]:
        copy.wait()

    for s in slots:
        gradient = grad[s]
        shaped = dot(lroot[s], gradient, ((1,), (0,)))
        shaped = dot(shaped, rroot[s], ((1,), (0,)))
        new_second = ADAM_DECAY * second[s] + (1.0 - ADAM_DECAY) * gradient * gradient
        out_second[0, 0, s] = new_second
        adam_step = gradient / jnp.sqrt(new_second)
        adam_norm = jnp.sqrt(jnp.sum(adam_step * adam_step, keepdims=True))
        shaped_norm = jnp.sqrt(jnp.sum(shaped * shaped, keepdims=True))
        scale = adam_norm / (shaped_norm + NORM_EPS)
        new_weights = weights[s] - LEARN_RATE * scale * shaped
        out_weights[0, 0, s] = new_weights
        gathered[me, s] = new_weights.astype(gathered.dtype)

    relay = outer >= 4
    out_head = pl.ds(0, out_cut)
    out_tail = pl.ds(out_cut, blocks.shape[1] - out_cut)

    def relayed(p, q, ends):
        return relay and (p, q) in [(0, outer - 1), (outer - 1, 0)][:ends]

    def targets_of(ends):
        def table(p):
            found = [q for q in range(outer) if q != p and not relayed(p, q, ends)]
            found.sort(key=lambda q: -abs(q - p))
            return found + [p] * (outer - 1 - len(found))

        return table

    def sources_of(p):
        found = [q for q in range(outer) if q != p]
        found.sort(key=lambda q: abs(q - p))
        if relay and p in (1, outer - 2):
            first = outer - 1 if p == 1 else 0
            found.remove(first)
            found.insert(0, first)
        return found

    def of_mine(table_of):
        rows = [table_of(p) for p in range(outer)]
        mine = []
        for column in zip(*rows):
            value = jnp.int32(column[0])
            for p in range(1, outer):
                value = jnp.where(z == p, column[p], value)
            mine.append(value)
        return mine

    here = y * 2 + x
    head_ends, tail_ends = 1, 2
    line_sources = of_mine(sources_of)
    plane_targets = [t + (t >= here).astype(jnp.int32) for t in range(3)]
    maybe_sent = []

    def maybe_remote(condition, part, send_sem, recv_sem, to):
        copy = pltpu.make_async_remote_copy(
            src_ref=part,
            dst_ref=part,
            send_sem=send_sem,
            recv_sem=recv_sem,
            device_id=to,
            device_id_type=MESH,
        )
        pl.when(condition)(copy.start)
        maybe_sent.append((condition, copy))

    def heads(o):
        return gathered.at[o, :, out_head]

    def tails(o, count=1):
        return gathered.at[pl.ds(o, count), :, out_tail]

    def await_part(part, sem):
        pltpu.make_async_remote_copy(
            src_ref=part,
            dst_ref=part,
            send_sem=own_send_sem.at[0],
            recv_sem=sem,
            device_id=(place(z, y, 1 - x), mp),
            device_id_type=MESH,
        ).wait_recv()

    def fan_heads(c, o):
        for t, q in enumerate(plane_targets):
            remote(
                heads(o), heads(o), fan_send_sem.at[c, t], head_recv_sem.at[o], (z * 4 + q, mp)
            )

    def along_line(part, send_sem, recv_sem, ends):
        for t, zz in enumerate(of_mine(targets_of(ends))):
            maybe_remote(zz != z, part, send_sem.at[t], recv_sem, (place(zz, y, x), mp))

    def pass_on(part, send_sem, recv_sem, ends):
        if relay and ends:
            middle = z == outer - 2
            end = jnp.int32(outer - 1)
            if ends == 2:
                middle = middle | (z == 1)
                end = jnp.where(z == 1, 0, end)
            maybe_remote(middle, part, send_sem, recv_sem, (place(end, y, x), mp))

    def stats(s):
        gradient = grad[s]
        out_left[0, 0, s] = STAT_DECAY * left[s] + (1.0 - STAT_DECAY) * dot(gradient, gradient, ((1,), (1,)))
        out_right[0, 0, s] = STAT_DECAY * right[s] + (1.0 - STAT_DECAY) * dot(
            gradient, gradient, ((0,), (0,))
        )

    along_line(heads(me), own_send_sem, head_recv_sem.at[me], head_ends)
    for t, q in enumerate(plane_targets):
        remote(tails(me), tails(me), tail_fan_sem.at[t], plane_tail_sem.at[here], (z * 4 + q, mp))
    fan_heads(0, me)
    for q in plane_targets:
        await_part(tails(z * 4 + q), plane_tail_sem.at[q])
    along_line(tails(z * 4, 4), tail_line_sem, line_tail_sem.at[z], tail_ends)
    for t, zz in enumerate(line_sources):
        o = place(zz, y, x)
        await_part(heads(o), head_recv_sem.at[o])
        if t == 0:
            pass_on(heads(o), relay_sem.at[0], head_recv_sem.at[o], head_ends)
        fan_heads(1 + t, o)
    for t, zz in enumerate(line_sources):
        await_part(tails(zz * 4, 4), line_tail_sem.at[zz])
        if t == 0:
            pass_on(tails(zz * 4, 4), relay_sem.at[1], line_tail_sem.at[zz], tail_ends)
    for s in slots:
        stats(s)
    for zz in [z] + line_sources:
        for q in plane_targets:
            await_part(heads(zz * 4 + q), head_recv_sem.at[zz * 4 + q])
    for condition, copy in maybe_sent:
        pl.when(condition)(copy.wait_send)

    for b in range(total):
        owner = owners[b]
        block = gathered[owner, jnp.where(table[0, owner] == b, 0, 1)]
        if b < values:
            out_values[b] = block
        else:
            out_keys[b - values] = block
    for copy in sent:
        copy.wait_send()


def store_kernel(*refs):
    half = (len(refs) - 1) // 2
    copies = [
        pltpu.make_async_copy(src, dst, refs[-1].at[i])
        for i, (src, dst) in enumerate(zip(refs[:half], refs[half:-1]))
    ]
    for copy in copies:
        copy.start()
    for copy in copies:
        copy.wait()


def on_device(value_grads, key_grads, owners, weights, left, right, left_root, right_root, second):
    dp_count = lax.axis_size("dp")
    mp_count = lax.axis_size("mp")
    capacity = weights.shape[2]
    values = value_grads.shape[1]
    side = value_grads.shape[2]
    share = key_grads.shape[2] // mp_count
    total = values + share
    outer = dp_count // 4
    f32, bf16 = jnp.float32, jnp.bfloat16
    block = (side, side)
    state = jax.ShapeDtypeStruct((1, 1, capacity) + block, f32)
    owner_ids = pltpu.with_memory_space_constraint(owners[:, 0], pltpu.HBM)
    hbm = pl.BlockSpec(memory_space=pl.ANY)
    vmem = pl.BlockSpec(memory_space=pltpu.VMEM)
    dma = pltpu.SemaphoreType.DMA
    peers = max(outer - 1, 1)
    others = max(mp_count - 1, 1)
    cut = side - side // 4
    out_cut = side - side * 2 // 8
    head, tail = (cut, side), (side - cut, side)
    results_shape = [state] * 4 + [
        jax.ShapeDtypeStruct((values,) + block, bf16),
        jax.ShapeDtypeStruct((share,) + block, bf16),
    ]
    results = pl.pallas_call(
        functools.partial(main_kernel, (dp_count, mp_count, values, share, capacity, cut, out_cut)),
        out_shape=results_shape,
        in_specs=[hbm] * 9,
        out_specs=[vmem] * 6,
        scratch_shapes=[
            pltpu.VMEM((dp_count, capacity) + block, bf16),
            pltpu.SMEM((total,), jnp.int32),
            pltpu.SMEM((2, dp_count), jnp.int32),
            pltpu.VMEM((total + 1,) + block, bf16),
            pltpu.VMEM((share,) + block, bf16),
            pltpu.VMEM((others, share) + block, bf16),
        ]
        + [pltpu.VMEM((capacity,) + block, f32)] * 6
        + [pltpu.VMEM((outer, 3, capacity) + head, bf16)] * 2
        + [pltpu.VMEM((peers, capacity) + head, bf16)] * 2
        + [pltpu.VMEM((peers, 4, capacity) + tail, bf16)] * 2
        + [pltpu.VMEM((3, capacity) + tail, bf16)] * 2
        + [pltpu.VMEM((capacity,) + block, f32)]
        + [dma((9,)), dma((others,)), dma((others,))]
        + [dma((outer, 3))] * 2
        + [dma((peers,))] * 4
        + [dma((3,))] * 2
        + [dma((peers,)), dma((outer, 3)), dma((3,)), dma((peers,)), dma((dp_count,)), dma((4,)), dma((outer,)), dma((2,)), pltpu.SemaphoreType.REGULAR],
        compiler_params=pltpu.CompilerParams(
            collective_id=0, has_side_effects=True, vmem_limit_bytes=32 * 1024 * 1024
        ),
    )(
        owner_ids,
        *(
            pltpu.with_memory_space_constraint(a, pltpu.HBM)
            for a in (value_grads, key_grads, weights, left, right, left_root, right_root, second)
        ),
    )
    return pl.pallas_call(
        store_kernel,
        out_shape=results_shape,
        in_specs=[hbm] * 6,
        out_specs=[hbm] * 6,
        scratch_shapes=[dma((6,))],
        compiler_params=pltpu.CompilerParams(vmem_limit_bytes=8 * 1024 * 1024),
    )(*results)


def solution(mesh):
    state = P("dp", "mp", None, None, None)
    return jax.shard_map(
        on_device,
        mesh=mesh,
        in_specs=(P("dp", "mp", None, None), state, P("mp", None)) + (state,) * 6,
        out_specs=(state,) * 4 + (P("mp", None, None),) * 2,
        check_vma=False,
    )
```

```python
import functools

import jax
import jax.numpy as jnp
from jax import lax
from jax.experimental import pallas as pl
from jax.experimental.pallas import tpu as pltpu
from jax.sharding import PartitionSpec as P

STAT_DECAY = 0.95
ADAM_DECAY = 0.95
LEARN_RATE = 0.1
NORM_EPS = 1e-06
MESH = pl.DeviceIdType.MESH
HIGH = lax.Precision.HIGHEST


def dot(a, b, contract):
    return lax.dot_general(
        a, b, ((contract[0], contract[1]), ((), ())), precision=HIGH, preferred_element_type=jnp.float32
    )


def main_kernel(
    dims,
    owners_hbm,
    value_hbm,
    key_hbm,
    weights_hbm,
    left_hbm,
    right_hbm,
    lroot_hbm,
    rroot_hbm,
    second_hbm,
    out_weights,
    out_left,
    out_right,
    out_second,
    out_values,
    out_keys,
    gathered,
    owners,
    table,
    blocks,
    key_mine,
    key_recv,
    weights,
    left,
    right,
    lroot,
    rroot,
    second,
    plane_send,
    plane_recv,
    line_send,
    line_recv,
    cross_send,
    cross_recv,
    back_send,
    back_recv,
    grad,
    load_sem,
    key_send_sem,
    key_recv_sem,
    plane_send_sem,
    plane_recv_sem,
    line_send_sem,
    line_recv_sem,
    cross_send_sem,
    cross_recv_sem,
    back_send_sem,
    back_recv_sem,
    own_send_sem,
    fan_send_sem,
    tail_fan_sem,
    tail_line_sem,
    head_recv_sem,
    plane_tail_sem,
    line_tail_sem,
    relay_sem,
    turn_sem,
):
    dp_count, mp_count, values, share, capacity, cut, out_cut = dims
    outer = dp_count // 4
    total = values + share
    me = lax.axis_index("dp")
    mp = lax.axis_index("mp")
    x = me % 2
    y = (me // 2) % 2
    z = me // 4
    f32 = jnp.float32
    slots = range(capacity)
    head = pl.ds(0, cut)
    tail = pl.ds(cut, blocks.shape[1] - cut)

    def place(zz, yy, xx):
        return zz * 4 + yy * 2 + xx

    plane = [(1 - y, 1 - x), (y, 1 - x), (1 - y, x)]
    far_first = sorted(range(1, outer), key=lambda k: -min(k, outer - k))
    order = [2, 3, 1] + [0] if outer == 4 else far_first + [0]

    owner_load = pltpu.make_async_copy(owners_hbm, owners, load_sem.at[8])
    owner_load.start()
    loads = [
        pltpu.make_async_copy(value_hbm.at[0], blocks.at[pl.ds(0, values)], load_sem.at[0]),
        pltpu.make_async_copy(
            key_hbm.at[0, 0, pl.ds(mp * share, share)], key_mine, load_sem.at[1]
        ),
    ]
    for i, (src, dst) in enumerate(
        (
            (weights_hbm, weights),
            (left_hbm, left),
            (right_hbm, right),
            (lroot_hbm, lroot),
            (rroot_hbm, rroot),
            (second_hbm, second),
        )
    ):
        loads.append(pltpu.make_async_copy(src.at[0, 0], dst, load_sem.at[2 + i]))
    for copy in loads[:2]:
        copy.start()
    sent = []

    barrier = pltpu.get_barrier_semaphore()
    partners = [(me, (mp + k) % mp_count) for k in range(1, mp_count)]
    partners += [(place(z, yy, xx), mp) for yy, xx in plane]
    partners += [(place((z + k) % outer, y, x), mp) for k in range(1, outer)]
    for partner in partners:
        pl.semaphore_signal(barrier, inc=1, device_id=partner, device_id_type=MESH)

    def remote(src, dst, send_sem, recv_sem, to):
        copy = pltpu.make_async_remote_copy(
            src_ref=src,
            dst_ref=dst,
            send_sem=send_sem,
            recv_sem=recv_sem,
            device_id=to,
            device_id_type=MESH,
        )
        copy.start()
        sent.append(copy)
        return copy

    pl.semaphore_wait(barrier, len(partners))

    key_copies = []
    for k in range(1, mp_count):
        to = (mp + k) % mp_count
        key_copies.append(
            remote(
                key_hbm.at[0, 0, pl.ds(to * share, share)],
                key_recv.at[k - 1],
                key_send_sem.at[k - 1],
                key_recv_sem.at[k - 1],
                (me, to),
            )
        )

    blocks[total] = jnp.zeros(blocks.shape[1:], blocks.dtype)
    owner_load.wait()

    def fill(o, carry):
        first = jnp.int32(total)
        last = jnp.int32(-1)
        for b in range(total):
            same = owners[b] == o
            first = jnp.minimum(first, jnp.where(same, b, total))
            last = jnp.maximum(last, jnp.where(same, b, -1))
        table[0, o] = first
        table[1, o] = jnp.where(last > first, last, total)
        return carry

    lax.fori_loop(0, dp_count, fill, 0)
    loads[0].wait()
    loads[1].wait()
    for copy in key_copies:
        copy.wait_recv()
    for j in range(share):
        key_sum = key_mine[j].astype(f32)
        for k in range(1, mp_count):
            key_sum = key_sum + key_recv[k - 1, j].astype(f32)
        blocks[values + j] = key_sum.astype(blocks.dtype)

    def of_mine(table_of):
        rows = [table_of(p) for p in range(outer)]
        mine = []
        for column in zip(*rows):
            value = jnp.int32(column[0])
            for p in range(1, outer):
                value = jnp.where(z == p, column[p], value)
            mine.append(value)
        return mine

    def sums_of(p):
        found = [q for q in range(outer) if q != p]
        found.sort(key=lambda q: (-abs(q - p), q))
        return found

    sum_order = of_mine(sums_of) + [z]

    plane_copies, cross_copies = {}, {}

    def start_plane(c):
        zz = sum_order[c]
        for q, (yy, xx) in enumerate(plane):
            for s in slots:
                plane_send[c, q, s] = blocks[table[s, place(zz, yy, xx)], head]
            plane_copies[c, q] = remote(
                plane_send.at[c, q],
                plane_recv.at[c, q],
                plane_send_sem.at[c, q],
                plane_recv_sem.at[c, q],
                (place(z, yy, xx), mp),
            )

    def start_cross(c):
        zz = sum_order[c]
        for q in range(4):
            for s in slots:
                cross_send[c, q, s] = blocks[table[s, zz * 4 + q], tail]
        cross_copies[c] = remote(
            cross_send.at[c],
            cross_recv.at[z],
            cross_send_sem.at[c],
            cross_recv_sem.at[z],
            (place(zz, y, x), mp),
        )

    if mp_count % 2 == 0:

        @pl.when(mp % 2 == 1)
        def _():
            pl.semaphore_wait(turn_sem, 1)

    for c in range(outer):
        start_plane(c)
        if c < outer - 1:
            start_cross(c)
    for copy in loads[2:]:
        copy.start()

    line_copies, back_copies = {}, {}

    def plane_sum(c, s):
        part = blocks[table[s, place(sum_order[c], y, x)], head].astype(f32)
        for q in range(3):
            part = part + plane_recv[c, q, s].astype(f32)
        return part

    def await_sum(src, dst, send_sem, recv_sem):
        pltpu.make_async_remote_copy(
            src_ref=src,
            dst_ref=dst,
            send_sem=send_sem,
            recv_sem=recv_sem,
            device_id=(place(z, y, 1 - x), mp),
            device_id_type=MESH,
        ).wait_recv()

    def start_line(c):
        for q in range(3):
            plane_copies[c, q].wait_recv()
        for s in slots:
            line_send[c, s] = plane_sum(c, s).astype(line_send.dtype)
        line_copies[c] = remote(
            line_send.at[c],
            line_recv.at[z],
            line_send_sem.at[c],
            line_recv_sem.at[z],
            (place(sum_order[c], y, x), mp),
        )

    def cross_sum(yy, xx, s):
        part = blocks[table[s, place(z, yy, xx)], tail].astype(f32)
        for c in range(outer - 1):
            part = part + cross_recv[sum_order[c], yy * 2 + xx, s].astype(f32)
        return part

    def start_back():
        for zz in sum_order[:-1]:
            await_sum(cross_send.at[0], cross_recv.at[zz], cross_send_sem.at[0], cross_recv_sem.at[zz])
        for q, (yy, xx) in enumerate(plane):
            for s in slots:
                back_send[q, s] = cross_sum(yy, xx, s).astype(back_send.dtype)
            back_copies[q] = remote(
                back_send.at[q],
                back_recv.at[q],
                back_send_sem.at[q],
                back_recv_sem.at[q],
                (place(z, yy, xx), mp),
            )

    half = outer // 2
    for c in range(half):
        start_line(c)
        if c == 0:
            if mp_count % 2 == 0:

                @pl.when(mp % 2 == 0)
                def _():
                    pl.semaphore_signal(turn_sem, inc=1, device_id=(me, mp + 1), device_id_type=MESH)
    start_back()
    for c in range(half, outer - 1):
        start_line(c)
    for q in range(3):
        plane_copies[outer - 1, q].wait_recv()
    for s in slots:
        grad[s, head] = plane_sum(outer - 1, s)
        grad[s, tail] = cross_sum(y, x, s)
    for q in range(3):
        back_copies[q].wait_recv()
    for s in slots:
        part = grad[s, tail]
        for q in range(3):
            part = part + back_recv[q, s].astype(f32)
        grad[s, tail] = part
    for zz in sum_order[:-1]:
        await_sum(line_send.at[0], line_recv.at[zz], line_send_sem.at[0], line_recv_sem.at[zz])
    for s in slots:
        part = grad[s, head]
        for c in range(outer - 1):
            part = part + line_recv[sum_order[c], s].astype(f32)
        grad[s, head] = part
    for copy in loads[2:]:
        copy.wait()

    for s in slots:
        gradient = grad[s]
        shaped = dot(lroot[s], gradient, ((1,), (0,)))
        shaped = dot(shaped, rroot[s], ((1,), (0,)))
        new_second = ADAM_DECAY * second[s] + (1.0 - ADAM_DECAY) * gradient * gradient
        out_second[0, 0, s] = new_second
        adam_step = gradient / jnp.sqrt(new_second)
        adam_norm = jnp.sqrt(jnp.sum(adam_step * adam_step, keepdims=True))
        shaped_norm = jnp.sqrt(jnp.sum(shaped * shaped, keepdims=True))
        scale = adam_norm / (shaped_norm + NORM_EPS)
        new_weights = weights[s] - LEARN_RATE * scale * shaped
        out_weights[0, 0, s] = new_weights
        gathered[me, s] = new_weights.astype(gathered.dtype)

    relay = outer >= 4
    out_head = pl.ds(0, out_cut)
    out_tail = pl.ds(out_cut, blocks.shape[1] - out_cut)

    def relayed(p, q, ends):
        return relay and (p, q) in [(0, outer - 1), (outer - 1, 0)][:ends]

    def targets_of(ends):
        def table(p):
            found = [q for q in range(outer) if q != p and not relayed(p, q, ends)]
            found.sort(key=lambda q: -abs(q - p))
            return found + [p] * (outer - 1 - len(found))

        return table

    def sources_of(p):
        found = [q for q in range(outer) if q != p]
        found.sort(key=lambda q: abs(q - p))
        if relay and p in (1, outer - 2):
            first = outer - 1 if p == 1 else 0
            found.remove(first)
            found.insert(0, first)
        return found

    here = y * 2 + x
    head_ends, tail_ends = 1, 2
    line_sources = of_mine(sources_of)
    plane_targets = [t + (t >= here).astype(jnp.int32) for t in range(3)]
    maybe_sent = []

    def maybe_remote(condition, part, send_sem, recv_sem, to):
        copy = pltpu.make_async_remote_copy(
            src_ref=part,
            dst_ref=part,
            send_sem=send_sem,
            recv_sem=recv_sem,
            device_id=to,
            device_id_type=MESH,
        )
        pl.when(condition)(copy.start)
        maybe_sent.append((condition, copy))

    def heads(o):
        return gathered.at[o, :, out_head]

    def tails(o, count=1):
        return gathered.at[pl.ds(o, count), :, out_tail]

    def await_part(part, sem):
        pltpu.make_async_remote_copy(
            src_ref=part,
            dst_ref=part,
            send_sem=own_send_sem.at[0],
            recv_sem=sem,
            device_id=(place(z, y, 1 - x), mp),
            device_id_type=MESH,
        ).wait_recv()

    def fan_heads(c, o):
        for t, q in enumerate(plane_targets):
            remote(
                heads(o), heads(o), fan_send_sem.at[c, t], head_recv_sem.at[o], (z * 4 + q, mp)
            )

    def along_line(part, send_sem, recv_sem, ends):
        for t, zz in enumerate(of_mine(targets_of(ends))):
            maybe_remote(zz != z, part, send_sem.at[t], recv_sem, (place(zz, y, x), mp))

    def pass_on(part, send_sem, recv_sem, ends):
        if relay and ends:
            middle = z == outer - 2
            end = jnp.int32(outer - 1)
            if ends == 2:
                middle = middle | (z == 1)
                end = jnp.where(z == 1, 0, end)
            maybe_remote(middle, part, send_sem, recv_sem, (place(end, y, x), mp))

    def stats(s):
        gradient = grad[s]
        out_left[0, 0, s] = STAT_DECAY * left[s] + (1.0 - STAT_DECAY) * dot(gradient, gradient, ((1,), (1,)))
        out_right[0, 0, s] = STAT_DECAY * right[s] + (1.0 - STAT_DECAY) * dot(
            gradient, gradient, ((0,), (0,))
        )

    for t, q in enumerate(plane_targets):
        remote(tails(me), tails(me), tail_fan_sem.at[t], plane_tail_sem.at[here], (z * 4 + q, mp))
    along_line(heads(me), own_send_sem, head_recv_sem.at[me], head_ends)
    fan_heads(0, me)
    for q in plane_targets:
        await_part(tails(z * 4 + q), plane_tail_sem.at[q])
    along_line(tails(z * 4, 4), tail_line_sem, line_tail_sem.at[z], tail_ends)
    for t, zz in enumerate(line_sources):
        o = place(zz, y, x)
        await_part(heads(o), head_recv_sem.at[o])
        if t == 0:
            pass_on(heads(o), relay_sem.at[0], head_recv_sem.at[o], head_ends)
        fan_heads(1 + t, o)
    for t, zz in enumerate(line_sources):
        await_part(tails(zz * 4, 4), line_tail_sem.at[zz])
        if t == 0:
            pass_on(tails(zz * 4, 4), relay_sem.at[1], line_tail_sem.at[zz], tail_ends)
    for s in slots:
        stats(s)
    for zz in [z] + line_sources:
        for q in plane_targets:
            await_part(heads(zz * 4 + q), head_recv_sem.at[zz * 4 + q])
    for condition, copy in maybe_sent:
        pl.when(condition)(copy.wait_send)

    for b in range(total):
        owner = owners[b]
        block = gathered[owner, jnp.where(table[0, owner] == b, 0, 1)]
        if b < values:
            out_values[b] = block
        else:
            out_keys[b - values] = block
    for copy in sent:
        copy.wait_send()


def store_kernel(*refs):
    half = (len(refs) - 1) // 2
    copies = [
        pltpu.make_async_copy(src, dst, refs[-1].at[i])
        for i, (src, dst) in enumerate(zip(refs[:half], refs[half:-1]))
    ]
    for copy in copies:
        copy.start()
    for copy in copies:
        copy.wait()


def on_device(value_grads, key_grads, owners, weights, left, right, left_root, right_root, second):
    dp_count = lax.axis_size("dp")
    mp_count = lax.axis_size("mp")
    capacity = weights.shape[2]
    values = value_grads.shape[1]
    side = value_grads.shape[2]
    share = key_grads.shape[2] // mp_count
    total = values + share
    outer = dp_count // 4
    f32, bf16 = jnp.float32, jnp.bfloat16
    block = (side, side)
    state = jax.ShapeDtypeStruct((1, 1, capacity) + block, f32)
    owner_ids = pltpu.with_memory_space_constraint(owners[:, 0], pltpu.HBM)
    hbm = pl.BlockSpec(memory_space=pl.ANY)
    vmem = pl.BlockSpec(memory_space=pltpu.VMEM)
    dma = pltpu.SemaphoreType.DMA
    peers = max(outer - 1, 1)
    others = max(mp_count - 1, 1)
    cut = side - side * 2 // 8
    out_cut = side - side * 2 // 8
    head, tail = (cut, side), (side - cut, side)
    results_shape = [state] * 4 + [
        jax.ShapeDtypeStruct((values,) + block, bf16),
        jax.ShapeDtypeStruct((share,) + block, bf16),
    ]
    results = pl.pallas_call(
        functools.partial(main_kernel, (dp_count, mp_count, values, share, capacity, cut, out_cut)),
        out_shape=results_shape,
        in_specs=[hbm] * 9,
        out_specs=[vmem] * 6,
        scratch_shapes=[
            pltpu.VMEM((dp_count, capacity) + block, bf16),
            pltpu.SMEM((total,), jnp.int32),
            pltpu.SMEM((2, dp_count), jnp.int32),
            pltpu.VMEM((total + 1,) + block, bf16),
            pltpu.VMEM((share,) + block, bf16),
            pltpu.VMEM((others, share) + block, bf16),
        ]
        + [pltpu.VMEM((capacity,) + block, f32)] * 6
        + [pltpu.VMEM((outer, 3, capacity) + head, bf16)] * 2
        + [pltpu.VMEM((peers, capacity) + head, bf16), pltpu.VMEM((outer, capacity) + head, bf16)]
        + [pltpu.VMEM((peers, 4, capacity) + tail, bf16), pltpu.VMEM((outer, 4, capacity) + tail, bf16)]
        + [pltpu.VMEM((3, capacity) + tail, bf16)] * 2
        + [pltpu.VMEM((capacity,) + block, f32)]
        + [dma((9,)), dma((others,)), dma((others,))]
        + [dma((outer, 3))] * 2
        + [dma((outer,))] * 4
        + [dma((3,))] * 2
        + [dma((peers,)), dma((outer, 3)), dma((3,)), dma((peers,)), dma((dp_count,)), dma((4,)), dma((outer,)), dma((2,)), pltpu.SemaphoreType.REGULAR],
        compiler_params=pltpu.CompilerParams(
            collective_id=0, has_side_effects=True, vmem_limit_bytes=32 * 1024 * 1024
        ),
    )(
        owner_ids,
        *(
            pltpu.with_memory_space_constraint(a, pltpu.HBM)
            for a in (value_grads, key_grads, weights, left, right, left_root, right_root, second)
        ),
    )
    return pl.pallas_call(
        store_kernel,
        out_shape=results_shape,
        in_specs=[hbm] * 6,
        out_specs=[hbm] * 6,
        scratch_shapes=[dma((6,))],
        compiler_params=pltpu.CompilerParams(vmem_limit_bytes=8 * 1024 * 1024),
    )(*results)


def solution(mesh):
    state = P("dp", "mp", None, None, None)
    return jax.shard_map(
        on_device,
        mesh=mesh,
        in_specs=(P("dp", "mp", None, None), state, P("mp", None)) + (state,) * 6,
        out_specs=(state,) * 4 + (P("mp", None, None),) * 2,
        check_vma=False,
    )
```

```python
import functools

import jax
import jax.numpy as jnp
from jax import lax
from jax.experimental import pallas as pl
from jax.experimental.pallas import tpu as pltpu
from jax.sharding import PartitionSpec as P

STAT_DECAY = 0.95
ADAM_DECAY = 0.95
LEARN_RATE = 0.1
NORM_EPS = 1e-06
MESH = pl.DeviceIdType.MESH
HIGH = lax.Precision.HIGHEST


def dot(a, b, contract):
    return lax.dot_general(
        a, b, ((contract[0], contract[1]), ((), ())), precision=HIGH, preferred_element_type=jnp.float32
    )


def main_kernel(
    dims,
    owners_hbm,
    value_hbm,
    key_hbm,
    weights_hbm,
    left_hbm,
    right_hbm,
    lroot_hbm,
    rroot_hbm,
    second_hbm,
    out_weights,
    out_left,
    out_right,
    out_second,
    out_values,
    out_keys,
    gathered,
    owners,
    table,
    blocks,
    key_mine,
    key_recv,
    weights,
    left,
    right,
    lroot,
    rroot,
    second,
    plane_send,
    plane_recv,
    line_send,
    line_recv,
    cross_send,
    cross_recv,
    back_send,
    back_recv,
    grad,
    load_sem,
    key_send_sem,
    key_recv_sem,
    plane_send_sem,
    plane_recv_sem,
    line_send_sem,
    line_recv_sem,
    cross_send_sem,
    cross_recv_sem,
    back_send_sem,
    back_recv_sem,
    own_send_sem,
    fan_send_sem,
    tail_fan_sem,
    tail_line_sem,
    head_recv_sem,
    plane_tail_sem,
    line_tail_sem,
    relay_sem,
    turn_sem,
):
    dp_count, mp_count, values, share, capacity, cut, out_cut = dims
    outer = dp_count // 4
    total = values + share
    me = lax.axis_index("dp")
    mp = lax.axis_index("mp")
    x = me % 2
    y = (me // 2) % 2
    z = me // 4
    f32 = jnp.float32
    slots = range(capacity)
    head = pl.ds(0, cut)
    tail = pl.ds(cut, blocks.shape[1] - cut)

    def place(zz, yy, xx):
        return zz * 4 + yy * 2 + xx

    plane = [(1 - y, 1 - x), (y, 1 - x), (1 - y, x)]
    far_first = sorted(range(1, outer), key=lambda k: -min(k, outer - k))
    order = [2, 3, 1] + [0] if outer == 4 else far_first + [0]

    owner_load = pltpu.make_async_copy(owners_hbm, owners, load_sem.at[8])
    owner_load.start()
    loads = [
        pltpu.make_async_copy(value_hbm.at[0], blocks.at[pl.ds(0, values)], load_sem.at[0]),
        pltpu.make_async_copy(
            key_hbm.at[0, 0, pl.ds(mp * share, share)], key_mine, load_sem.at[1]
        ),
    ]
    for i, (src, dst) in enumerate(
        (
            (weights_hbm, weights),
            (left_hbm, left),
            (right_hbm, right),
            (lroot_hbm, lroot),
            (rroot_hbm, rroot),
            (second_hbm, second),
        )
    ):
        loads.append(pltpu.make_async_copy(src.at[0, 0], dst, load_sem.at[2 + i]))
    for copy in loads[:2]:
        copy.start()
    sent = []

    barrier = pltpu.get_barrier_semaphore()
    partners = [(me, (mp + k) % mp_count) for k in range(1, mp_count)]
    partners += [(place(z, yy, xx), mp) for yy, xx in plane]
    partners += [(place((z + k) % outer, y, x), mp) for k in range(1, outer)]
    for partner in partners:
        pl.semaphore_signal(barrier, inc=1, device_id=partner, device_id_type=MESH)

    def remote(src, dst, send_sem, recv_sem, to):
        copy = pltpu.make_async_remote_copy(
            src_ref=src,
            dst_ref=dst,
            send_sem=send_sem,
            recv_sem=recv_sem,
            device_id=to,
            device_id_type=MESH,
        )
        copy.start()
        sent.append(copy)
        return copy

    pl.semaphore_wait(barrier, len(partners))

    key_copies = []
    for k in range(1, mp_count):
        to = (mp + k) % mp_count
        key_copies.append(
            remote(
                key_hbm.at[0, 0, pl.ds(to * share, share)],
                key_recv.at[k - 1],
                key_send_sem.at[k - 1],
                key_recv_sem.at[k - 1],
                (me, to),
            )
        )

    blocks[total] = jnp.zeros(blocks.shape[1:], blocks.dtype)
    owner_load.wait()

    def fill(o, carry):
        first = jnp.int32(total)
        last = jnp.int32(-1)
        for b in range(total):
            same = owners[b] == o
            first = jnp.minimum(first, jnp.where(same, b, total))
            last = jnp.maximum(last, jnp.where(same, b, -1))
        table[0, o] = first
        table[1, o] = jnp.where(last > first, last, total)
        return carry

    lax.fori_loop(0, dp_count, fill, 0)
    loads[0].wait()
    loads[1].wait()
    for copy in key_copies:
        copy.wait_recv()
    for j in range(share):
        key_sum = key_mine[j].astype(f32)
        for k in range(1, mp_count):
            key_sum = key_sum + key_recv[k - 1, j].astype(f32)
        blocks[values + j] = key_sum.astype(blocks.dtype)

    def of_mine(table_of):
        rows = [table_of(p) for p in range(outer)]
        mine = []
        for column in zip(*rows):
            value = jnp.int32(column[0])
            for p in range(1, outer):
                value = jnp.where(z == p, column[p], value)
            mine.append(value)
        return mine

    def sums_of(p):
        found = [q for q in range(outer) if q != p]
        found.sort(key=lambda q: (-abs(q - p), q))
        return found

    sum_order = of_mine(sums_of) + [z]

    plane_copies, cross_copies = {}, {}

    def start_plane(c):
        zz = sum_order[c]
        for q, (yy, xx) in enumerate(plane):
            for s in slots:
                plane_send[c, q, s] = blocks[table[s, place(zz, yy, xx)], head]
            plane_copies[c, q] = remote(
                plane_send.at[c, q],
                plane_recv.at[c, q],
                plane_send_sem.at[c, q],
                plane_recv_sem.at[c, q],
                (place(z, yy, xx), mp),
            )

    def start_cross(c):
        zz = sum_order[c]
        for q in range(4):
            for s in slots:
                cross_send[c, q, s] = blocks[table[s, zz * 4 + q], tail]
        cross_copies[c] = remote(
            cross_send.at[c],
            cross_recv.at[z],
            cross_send_sem.at[c],
            cross_recv_sem.at[z],
            (place(zz, y, x), mp),
        )

    if mp_count % 2 == 0:

        @pl.when(mp % 2 == 1)
        def _():
            pl.semaphore_wait(turn_sem, 1)

    start_cross(0)
    start_plane(0)
    for c in range(1, outer):
        if c < outer - 1:
            start_cross(c)
        start_plane(c)
    for copy in loads[2:]:
        copy.start()

    line_copies, back_copies = {}, {}

    def plane_sum(c, s):
        part = blocks[table[s, place(sum_order[c], y, x)], head].astype(f32)
        for q in range(3):
            part = part + plane_recv[c, q, s].astype(f32)
        return part

    def await_sum(src, dst, send_sem, recv_sem):
        pltpu.make_async_remote_copy(
            src_ref=src,
            dst_ref=dst,
            send_sem=send_sem,
            recv_sem=recv_sem,
            device_id=(place(z, y, 1 - x), mp),
            device_id_type=MESH,
        ).wait_recv()

    def start_line(c):
        for q in range(3):
            if (c, q) != (0, 1):
                plane_copies[c, q].wait_recv()
        for s in slots:
            line_send[c, s] = plane_sum(c, s).astype(line_send.dtype)
        line_copies[c] = remote(
            line_send.at[c],
            line_recv.at[z],
            line_send_sem.at[c],
            line_recv_sem.at[z],
            (place(sum_order[c], y, x), mp),
        )

    def cross_sum(yy, xx, s):
        part = blocks[table[s, place(z, yy, xx)], tail].astype(f32)
        for c in range(outer - 1):
            part = part + cross_recv[sum_order[c], yy * 2 + xx, s].astype(f32)
        return part

    def start_back():
        for zz in sum_order[:-1]:
            await_sum(cross_send.at[0], cross_recv.at[zz], cross_send_sem.at[0], cross_recv_sem.at[zz])
        for q, (yy, xx) in enumerate(plane):
            for s in slots:
                back_send[q, s] = cross_sum(yy, xx, s).astype(back_send.dtype)
            back_copies[q] = remote(
                back_send.at[q],
                back_recv.at[q],
                back_send_sem.at[q],
                back_recv_sem.at[q],
                (place(z, yy, xx), mp),
            )

    plane_copies[0, 1].wait_recv()
    if mp_count % 2 == 0:

        @pl.when(mp % 2 == 0)
        def _():
            pl.semaphore_signal(turn_sem, inc=1, device_id=(me, mp + 1), device_id_type=MESH)

    half = outer // 2
    for c in range(half):
        start_line(c)
    start_back()
    for c in range(half, outer - 1):
        start_line(c)
    for q in range(3):
        plane_copies[outer - 1, q].wait_recv()
    for s in slots:
        grad[s, head] = plane_sum(outer - 1, s)
        grad[s, tail] = cross_sum(y, x, s)
    for q in range(3):
        back_copies[q].wait_recv()
    for s in slots:
        part = grad[s, tail]
        for q in range(3):
            part = part + back_recv[q, s].astype(f32)
        grad[s, tail] = part
    for zz in sum_order[:-1]:
        await_sum(line_send.at[0], line_recv.at[zz], line_send_sem.at[0], line_recv_sem.at[zz])
    for s in slots:
        part = grad[s, head]
        for c in range(outer - 1):
            part = part + line_recv[sum_order[c], s].astype(f32)
        grad[s, head] = part
    for copy in loads[2:]:
        copy.wait()

    for s in slots:
        gradient = grad[s]
        shaped = dot(lroot[s], gradient, ((1,), (0,)))
        shaped = dot(shaped, rroot[s], ((1,), (0,)))
        new_second = ADAM_DECAY * second[s] + (1.0 - ADAM_DECAY) * gradient * gradient
        out_second[0, 0, s] = new_second
        adam_step = gradient / jnp.sqrt(new_second)
        adam_norm = jnp.sqrt(jnp.sum(adam_step * adam_step, keepdims=True))
        shaped_norm = jnp.sqrt(jnp.sum(shaped * shaped, keepdims=True))
        scale = adam_norm / (shaped_norm + NORM_EPS)
        new_weights = weights[s] - LEARN_RATE * scale * shaped
        out_weights[0, 0, s] = new_weights
        gathered[me, s] = new_weights.astype(gathered.dtype)

    relay = outer >= 4
    out_head = pl.ds(0, out_cut)
    out_tail = pl.ds(out_cut, blocks.shape[1] - out_cut)

    def relayed(p, q, ends):
        return relay and (p, q) in [(0, outer - 1), (outer - 1, 0)][:ends]

    def targets_of(ends):
        def table(p):
            found = [q for q in range(outer) if q != p and not relayed(p, q, ends)]
            found.sort(key=lambda q: -abs(q - p))
            return found + [p] * (outer - 1 - len(found))

        return table

    def sources_of(p):
        found = [q for q in range(outer) if q != p]
        found.sort(key=lambda q: abs(q - p))
        if relay and p in (1, outer - 2):
            first = outer - 1 if p == 1 else 0
            found.remove(first)
            found.insert(0, first)
        return found

    here = y * 2 + x
    head_ends, tail_ends = 1, 2
    line_sources = of_mine(sources_of)
    plane_targets = [t + (t >= here).astype(jnp.int32) for t in range(3)]
    maybe_sent = []

    def maybe_remote(condition, part, send_sem, recv_sem, to):
        copy = pltpu.make_async_remote_copy(
            src_ref=part,
            dst_ref=part,
            send_sem=send_sem,
            recv_sem=recv_sem,
            device_id=to,
            device_id_type=MESH,
        )
        pl.when(condition)(copy.start)
        maybe_sent.append((condition, copy))

    def heads(o):
        return gathered.at[o, :, out_head]

    def tails(o, count=1):
        return gathered.at[pl.ds(o, count), :, out_tail]

    def await_part(part, sem):
        pltpu.make_async_remote_copy(
            src_ref=part,
            dst_ref=part,
            send_sem=own_send_sem.at[0],
            recv_sem=sem,
            device_id=(place(z, y, 1 - x), mp),
            device_id_type=MESH,
        ).wait_recv()

    def fan_heads(c, o):
        for t, q in enumerate(plane_targets):
            remote(
                heads(o), heads(o), fan_send_sem.at[c, t], head_recv_sem.at[o], (z * 4 + q, mp)
            )

    def along_line(part, send_sem, recv_sem, ends):
        for t, zz in enumerate(of_mine(targets_of(ends))):
            maybe_remote(zz != z, part, send_sem.at[t], recv_sem, (place(zz, y, x), mp))

    def pass_on(part, send_sem, recv_sem, ends):
        if relay and ends:
            middle = z == outer - 2
            end = jnp.int32(outer - 1)
            if ends == 2:
                middle = middle | (z == 1)
                end = jnp.where(z == 1, 0, end)
            maybe_remote(middle, part, send_sem, recv_sem, (place(end, y, x), mp))

    def stats(s):
        gradient = grad[s]
        out_left[0, 0, s] = STAT_DECAY * left[s] + (1.0 - STAT_DECAY) * dot(gradient, gradient, ((1,), (1,)))
        out_right[0, 0, s] = STAT_DECAY * right[s] + (1.0 - STAT_DECAY) * dot(
            gradient, gradient, ((0,), (0,))
        )

    for t, q in enumerate(plane_targets):
        remote(tails(me), tails(me), tail_fan_sem.at[t], plane_tail_sem.at[here], (z * 4 + q, mp))
    along_line(heads(me), own_send_sem, head_recv_sem.at[me], head_ends)
    fan_heads(0, me)
    for q in plane_targets:
        await_part(tails(z * 4 + q), plane_tail_sem.at[q])
    along_line(tails(z * 4, 4), tail_line_sem, line_tail_sem.at[z], tail_ends)
    for t, zz in enumerate(line_sources):
        o = place(zz, y, x)
        await_part(heads(o), head_recv_sem.at[o])
        if t == 0:
            pass_on(heads(o), relay_sem.at[0], head_recv_sem.at[o], head_ends)
        fan_heads(1 + t, o)
    for t, zz in enumerate(line_sources):
        await_part(tails(zz * 4, 4), line_tail_sem.at[zz])
        if t == 0:
            pass_on(tails(zz * 4, 4), relay_sem.at[1], line_tail_sem.at[zz], tail_ends)
    for s in slots:
        stats(s)
    for zz in [z] + line_sources:
        for q in plane_targets:
            await_part(heads(zz * 4 + q), head_recv_sem.at[zz * 4 + q])
    for condition, copy in maybe_sent:
        pl.when(condition)(copy.wait_send)

    for b in range(total):
        owner = owners[b]
        block = gathered[owner, jnp.where(table[0, owner] == b, 0, 1)]
        if b < values:
            out_values[b] = block
        else:
            out_keys[b - values] = block
    for copy in sent:
        copy.wait_send()


def store_kernel(*refs):
    half = (len(refs) - 1) // 2
    copies = [
        pltpu.make_async_copy(src, dst, refs[-1].at[i])
        for i, (src, dst) in enumerate(zip(refs[:half], refs[half:-1]))
    ]
    for copy in copies:
        copy.start()
    for copy in copies:
        copy.wait()


def on_device(value_grads, key_grads, owners, weights, left, right, left_root, right_root, second):
    dp_count = lax.axis_size("dp")
    mp_count = lax.axis_size("mp")
    capacity = weights.shape[2]
    values = value_grads.shape[1]
    side = value_grads.shape[2]
    share = key_grads.shape[2] // mp_count
    total = values + share
    outer = dp_count // 4
    f32, bf16 = jnp.float32, jnp.bfloat16
    block = (side, side)
    state = jax.ShapeDtypeStruct((1, 1, capacity) + block, f32)
    owner_ids = pltpu.with_memory_space_constraint(owners[:, 0], pltpu.HBM)
    hbm = pl.BlockSpec(memory_space=pl.ANY)
    vmem = pl.BlockSpec(memory_space=pltpu.VMEM)
    dma = pltpu.SemaphoreType.DMA
    peers = max(outer - 1, 1)
    others = max(mp_count - 1, 1)
    cut = side - side * 2 // 8
    out_cut = side - side * 2 // 8
    head, tail = (cut, side), (side - cut, side)
    results_shape = [state] * 4 + [
        jax.ShapeDtypeStruct((values,) + block, bf16),
        jax.ShapeDtypeStruct((share,) + block, bf16),
    ]
    results = pl.pallas_call(
        functools.partial(main_kernel, (dp_count, mp_count, values, share, capacity, cut, out_cut)),
        out_shape=results_shape,
        in_specs=[hbm] * 9,
        out_specs=[vmem] * 6,
        scratch_shapes=[
            pltpu.VMEM((dp_count, capacity) + block, bf16),
            pltpu.SMEM((total,), jnp.int32),
            pltpu.SMEM((2, dp_count), jnp.int32),
            pltpu.VMEM((total + 1,) + block, bf16),
            pltpu.VMEM((share,) + block, bf16),
            pltpu.VMEM((others, share) + block, bf16),
        ]
        + [pltpu.VMEM((capacity,) + block, f32)] * 6
        + [pltpu.VMEM((outer, 3, capacity) + head, bf16)] * 2
        + [pltpu.VMEM((peers, capacity) + head, bf16), pltpu.VMEM((outer, capacity) + head, bf16)]
        + [pltpu.VMEM((peers, 4, capacity) + tail, bf16), pltpu.VMEM((outer, 4, capacity) + tail, bf16)]
        + [pltpu.VMEM((3, capacity) + tail, bf16)] * 2
        + [pltpu.VMEM((capacity,) + block, f32)]
        + [dma((9,)), dma((others,)), dma((others,))]
        + [dma((outer, 3))] * 2
        + [dma((outer,))] * 4
        + [dma((3,))] * 2
        + [dma((peers,)), dma((outer, 3)), dma((3,)), dma((peers,)), dma((dp_count,)), dma((4,)), dma((outer,)), dma((2,)), pltpu.SemaphoreType.REGULAR],
        compiler_params=pltpu.CompilerParams(
            collective_id=0, has_side_effects=True, vmem_limit_bytes=32 * 1024 * 1024
        ),
    )(
        owner_ids,
        *(
            pltpu.with_memory_space_constraint(a, pltpu.HBM)
            for a in (value_grads, key_grads, weights, left, right, left_root, right_root, second)
        ),
    )
    return pl.pallas_call(
        store_kernel,
        out_shape=results_shape,
        in_specs=[hbm] * 6,
        out_specs=[hbm] * 6,
        scratch_shapes=[dma((6,))],
        compiler_params=pltpu.CompilerParams(vmem_limit_bytes=8 * 1024 * 1024),
    )(*results)


def solution(mesh):
    state = P("dp", "mp", None, None, None)
    return jax.shard_map(
        on_device,
        mesh=mesh,
        in_specs=(P("dp", "mp", None, None), state, P("mp", None)) + (state,) * 6,
        out_specs=(state,) * 4 + (P("mp", None, None),) * 2,
        check_vma=False,
    )
```

```python
import functools

import jax
import jax.numpy as jnp
from jax import lax
from jax.experimental import pallas as pl
from jax.experimental.pallas import tpu as pltpu
from jax.sharding import PartitionSpec as P

STAT_DECAY = 0.95
ADAM_DECAY = 0.95
LEARN_RATE = 0.1
NORM_EPS = 1e-06
MESH = pl.DeviceIdType.MESH
HIGH = lax.Precision.HIGHEST


def dot(a, b, contract):
    return lax.dot_general(
        a, b, ((contract[0], contract[1]), ((), ())), precision=HIGH, preferred_element_type=jnp.float32
    )


def split(a):
    high = a.astype(jnp.bfloat16)
    return high, (a - high.astype(jnp.float32)).astype(jnp.bfloat16)


def split_dot(a, b):
    (ah, al), (bh, bl) = a, b

    def one(p, q):
        return jnp.dot(p, q, preferred_element_type=jnp.float32)

    return one(ah, bh) + (one(ah, bl) + one(al, bh))


def main_kernel(
    dims,
    owners_hbm,
    value_hbm,
    key_hbm,
    weights_hbm,
    left_hbm,
    right_hbm,
    lroot_hbm,
    rroot_hbm,
    second_hbm,
    out_weights,
    out_left,
    out_right,
    out_second,
    out_values,
    out_keys,
    gathered,
    owners,
    table,
    blocks,
    key_mine,
    key_recv,
    weights,
    left,
    right,
    lroot,
    rroot,
    second,
    plane_send,
    plane_recv,
    line_send,
    line_recv,
    cross_send,
    cross_recv,
    back_send,
    back_recv,
    grad,
    load_sem,
    key_send_sem,
    key_recv_sem,
    plane_send_sem,
    plane_recv_sem,
    line_send_sem,
    line_recv_sem,
    cross_send_sem,
    cross_recv_sem,
    back_send_sem,
    back_recv_sem,
    own_send_sem,
    fan_send_sem,
    tail_fan_sem,
    tail_line_sem,
    head_recv_sem,
    plane_tail_sem,
    line_tail_sem,
    relay_sem,
    turn_sem,
):
    dp_count, mp_count, values, share, capacity, cut, out_cut = dims
    outer = dp_count // 4
    total = values + share
    me = lax.axis_index("dp")
    mp = lax.axis_index("mp")
    x = me % 2
    y = (me // 2) % 2
    z = me // 4
    f32 = jnp.float32
    slots = range(capacity)
    head = pl.ds(0, cut)
    tail = pl.ds(cut, blocks.shape[1] - cut)

    def place(zz, yy, xx):
        return zz * 4 + yy * 2 + xx

    plane = [(1 - y, 1 - x), (y, 1 - x), (1 - y, x)]
    far_first = sorted(range(1, outer), key=lambda k: -min(k, outer - k))
    order = [2, 3, 1] + [0] if outer == 4 else far_first + [0]

    owner_load = pltpu.make_async_copy(owners_hbm, owners, load_sem.at[8])
    owner_load.start()
    loads = [
        pltpu.make_async_copy(value_hbm.at[0], blocks.at[pl.ds(0, values)], load_sem.at[0]),
        pltpu.make_async_copy(
            key_hbm.at[0, 0, pl.ds(mp * share, share)], key_mine, load_sem.at[1]
        ),
    ]
    for i, (src, dst) in enumerate(
        (
            (weights_hbm, weights),
            (left_hbm, left),
            (right_hbm, right),
            (lroot_hbm, lroot),
            (rroot_hbm, rroot),
            (second_hbm, second),
        )
    ):
        loads.append(pltpu.make_async_copy(src.at[0, 0], dst, load_sem.at[2 + i]))
    for copy in loads[:2]:
        copy.start()
    sent = []

    barrier = pltpu.get_barrier_semaphore()
    partners = [(me, (mp + k) % mp_count) for k in range(1, mp_count)]
    partners += [(place(z, yy, xx), mp) for yy, xx in plane]
    partners += [(place((z + k) % outer, y, x), mp) for k in range(1, outer)]
    for partner in partners:
        pl.semaphore_signal(barrier, inc=1, device_id=partner, device_id_type=MESH)

    def remote(src, dst, send_sem, recv_sem, to):
        copy = pltpu.make_async_remote_copy(
            src_ref=src,
            dst_ref=dst,
            send_sem=send_sem,
            recv_sem=recv_sem,
            device_id=to,
            device_id_type=MESH,
        )
        copy.start()
        sent.append(copy)
        return copy

    pl.semaphore_wait(barrier, len(partners))

    key_copies = []
    for k in range(1, mp_count):
        to = (mp + k) % mp_count
        key_copies.append(
            remote(
                key_hbm.at[0, 0, pl.ds(to * share, share)],
                key_recv.at[k - 1],
                key_send_sem.at[k - 1],
                key_recv_sem.at[k - 1],
                (me, to),
            )
        )

    blocks[total] = jnp.zeros(blocks.shape[1:], blocks.dtype)
    owner_load.wait()

    def fill(o, carry):
        first = jnp.int32(total)
        last = jnp.int32(-1)
        for b in range(total):
            same = owners[b] == o
            first = jnp.minimum(first, jnp.where(same, b, total))
            last = jnp.maximum(last, jnp.where(same, b, -1))
        table[0, o] = first
        table[1, o] = jnp.where(last > first, last, total)
        return carry

    lax.fori_loop(0, dp_count, fill, 0)
    loads[0].wait()
    loads[1].wait()
    for copy in key_copies:
        copy.wait_recv()
    for j in range(share):
        key_sum = key_mine[j].astype(f32)
        for k in range(1, mp_count):
            key_sum = key_sum + key_recv[k - 1, j].astype(f32)
        blocks[values + j] = key_sum.astype(blocks.dtype)

    def of_mine(table_of):
        rows = [table_of(p) for p in range(outer)]
        mine = []
        for column in zip(*rows):
            value = jnp.int32(column[0])
            for p in range(1, outer):
                value = jnp.where(z == p, column[p], value)
            mine.append(value)
        return mine

    def sums_of(p):
        found = [q for q in range(outer) if q != p]
        found.sort(key=lambda q: (-abs(q - p), q))
        return found

    sum_order = of_mine(sums_of) + [z]

    plane_copies, cross_copies = {}, {}

    def start_plane(c):
        zz = sum_order[c]
        for q, (yy, xx) in enumerate(plane):
            for s in slots:
                plane_send[c, q, s] = blocks[table[s, place(zz, yy, xx)], head]
            plane_copies[c, q] = remote(
                plane_send.at[c, q],
                plane_recv.at[c, q],
                plane_send_sem.at[c, q],
                plane_recv_sem.at[c, q],
                (place(z, yy, xx), mp),
            )

    def start_cross(c):
        zz = sum_order[c]
        for q in range(4):
            for s in slots:
                cross_send[c, q, s] = blocks[table[s, zz * 4 + q], tail]
        cross_copies[c] = remote(
            cross_send.at[c],
            cross_recv.at[z],
            cross_send_sem.at[c],
            cross_recv_sem.at[z],
            (place(zz, y, x), mp),
        )

    if mp_count % 2 == 0:

        @pl.when(mp % 2 == 1)
        def _():
            pl.semaphore_wait(turn_sem, 1)

    for c in range(outer):
        start_plane(c)
        if c < outer - 1:
            start_cross(c)
    for copy in loads[2:]:
        copy.start()

    line_copies, back_copies = {}, {}

    def plane_sum(c, s):
        part = blocks[table[s, place(sum_order[c], y, x)], head].astype(f32)
        for q in range(3):
            part = part + plane_recv[c, q, s].astype(f32)
        return part

    def await_sum(src, dst, send_sem, recv_sem):
        pltpu.make_async_remote_copy(
            src_ref=src,
            dst_ref=dst,
            send_sem=send_sem,
            recv_sem=recv_sem,
            device_id=(place(z, y, 1 - x), mp),
            device_id_type=MESH,
        ).wait_recv()

    def start_line(c):
        for q in range(3):
            plane_copies[c, q].wait_recv()
        for s in slots:
            line_send[c, s] = plane_sum(c, s).astype(line_send.dtype)
        line_copies[c] = remote(
            line_send.at[c],
            line_recv.at[z],
            line_send_sem.at[c],
            line_recv_sem.at[z],
            (place(sum_order[c], y, x), mp),
        )

    def cross_sum(yy, xx, s):
        part = blocks[table[s, place(z, yy, xx)], tail].astype(f32)
        for c in range(outer - 1):
            part = part + cross_recv[sum_order[c], yy * 2 + xx, s].astype(f32)
        return part

    def start_back():
        for zz in sum_order[:-1]:
            await_sum(cross_send.at[0], cross_recv.at[zz], cross_send_sem.at[0], cross_recv_sem.at[zz])
        for q, (yy, xx) in enumerate(plane):
            for s in slots:
                back_send[q, s] = cross_sum(yy, xx, s).astype(back_send.dtype)
            back_copies[q] = remote(
                back_send.at[q],
                back_recv.at[q],
                back_send_sem.at[q],
                back_recv_sem.at[q],
                (place(z, yy, xx), mp),
            )

    half = outer // 2
    for c in range(half):
        start_line(c)
        if c == 0:
            if mp_count % 2 == 0:

                @pl.when(mp % 2 == 0)
                def _():
                    pl.semaphore_signal(turn_sem, inc=1, device_id=(me, mp + 1), device_id_type=MESH)
    start_back()
    for c in range(half, outer - 1):
        start_line(c)
    for q in range(3):
        plane_copies[outer - 1, q].wait_recv()
    for s in slots:
        grad[s, head] = plane_sum(outer - 1, s)
        grad[s, tail] = cross_sum(y, x, s)
    for q in range(3):
        back_copies[q].wait_recv()
    for s in slots:
        part = grad[s, tail]
        for q in range(3):
            part = part + back_recv[q, s].astype(f32)
        grad[s, tail] = part
    for zz in sum_order[:-1]:
        await_sum(line_send.at[0], line_recv.at[zz], line_send_sem.at[0], line_recv_sem.at[zz])
    for s in slots:
        part = grad[s, head]
        for c in range(outer - 1):
            part = part + line_recv[sum_order[c], s].astype(f32)
        grad[s, head] = part
    for copy in loads[2:]:
        copy.wait()

    for s in slots:
        gradient = grad[s]
        shaped = split_dot(split(lroot[s]), split(gradient))
        shaped = split_dot(split(shaped), split(rroot[s]))
        new_second = ADAM_DECAY * second[s] + (1.0 - ADAM_DECAY) * gradient * gradient
        out_second[0, 0, s] = new_second
        adam_step = gradient / jnp.sqrt(new_second)
        adam_norm = jnp.sqrt(jnp.sum(adam_step * adam_step, keepdims=True))
        shaped_norm = jnp.sqrt(jnp.sum(shaped * shaped, keepdims=True))
        scale = adam_norm / (shaped_norm + NORM_EPS)
        new_weights = weights[s] - LEARN_RATE * scale * shaped
        out_weights[0, 0, s] = new_weights
        gathered[me, s] = new_weights.astype(gathered.dtype)

    relay = outer >= 4
    out_head = pl.ds(0, out_cut)
    out_tail = pl.ds(out_cut, blocks.shape[1] - out_cut)

    def relayed(p, q, ends):
        return relay and (p, q) in [(0, outer - 1), (outer - 1, 0)][:ends]

    def targets_of(ends):
        def table(p):
            found = [q for q in range(outer) if q != p and not relayed(p, q, ends)]
            found.sort(key=lambda q: -abs(q - p))
            return found + [p] * (outer - 1 - len(found))

        return table

    def sources_of(p):
        found = [q for q in range(outer) if q != p]
        found.sort(key=lambda q: abs(q - p))
        if relay and p in (1, outer - 2):
            first = outer - 1 if p == 1 else 0
            found.remove(first)
            found.insert(0, first)
        return found

    here = y * 2 + x
    head_ends, tail_ends = 1, 2
    line_sources = of_mine(sources_of)
    plane_targets = [t + (t >= here).astype(jnp.int32) for t in range(3)]
    maybe_sent = []

    def maybe_remote(condition, part, send_sem, recv_sem, to):
        copy = pltpu.make_async_remote_copy(
            src_ref=part,
            dst_ref=part,
            send_sem=send_sem,
            recv_sem=recv_sem,
            device_id=to,
            device_id_type=MESH,
        )
        pl.when(condition)(copy.start)
        maybe_sent.append((condition, copy))

    def heads(o):
        return gathered.at[o, :, out_head]

    def tails(o, count=1):
        return gathered.at[pl.ds(o, count), :, out_tail]

    def await_part(part, sem):
        pltpu.make_async_remote_copy(
            src_ref=part,
            dst_ref=part,
            send_sem=own_send_sem.at[0],
            recv_sem=sem,
            device_id=(place(z, y, 1 - x), mp),
            device_id_type=MESH,
        ).wait_recv()

    def fan_heads(c, o):
        for t, q in enumerate(plane_targets):
            remote(
                heads(o), heads(o), fan_send_sem.at[c, t], head_recv_sem.at[o], (z * 4 + q, mp)
            )

    def along_line(part, send_sem, recv_sem, ends):
        for t, zz in enumerate(of_mine(targets_of(ends))):
            maybe_remote(zz != z, part, send_sem.at[t], recv_sem, (place(zz, y, x), mp))

    def pass_on(part, send_sem, recv_sem, ends):
        if relay and ends:
            middle = z == outer - 2
            end = jnp.int32(outer - 1)
            if ends == 2:
                middle = middle | (z == 1)
                end = jnp.where(z == 1, 0, end)
            maybe_remote(middle, part, send_sem, recv_sem, (place(end, y, x), mp))

    def stats(s):
        gradient = grad[s]
        out_left[0, 0, s] = STAT_DECAY * left[s] + (1.0 - STAT_DECAY) * dot(gradient, gradient, ((1,), (1,)))
        out_right[0, 0, s] = STAT_DECAY * right[s] + (1.0 - STAT_DECAY) * dot(
            gradient, gradient, ((0,), (0,))
        )

    for t, q in enumerate(plane_targets):
        remote(tails(me), tails(me), tail_fan_sem.at[t], plane_tail_sem.at[here], (z * 4 + q, mp))
    along_line(heads(me), own_send_sem, head_recv_sem.at[me], head_ends)
    fan_heads(0, me)
    for q in plane_targets:
        await_part(tails(z * 4 + q), plane_tail_sem.at[q])
    along_line(tails(z * 4, 4), tail_line_sem, line_tail_sem.at[z], tail_ends)
    for t, zz in enumerate(line_sources):
        o = place(zz, y, x)
        await_part(heads(o), head_recv_sem.at[o])
        if t == 0:
            pass_on(heads(o), relay_sem.at[0], head_recv_sem.at[o], head_ends)
        fan_heads(1 + t, o)
    for t, zz in enumerate(line_sources):
        await_part(tails(zz * 4, 4), line_tail_sem.at[zz])
        if t == 0:
            pass_on(tails(zz * 4, 4), relay_sem.at[1], line_tail_sem.at[zz], tail_ends)
    for s in slots:
        stats(s)
    for zz in [z] + line_sources:
        for q in plane_targets:
            await_part(heads(zz * 4 + q), head_recv_sem.at[zz * 4 + q])
    for condition, copy in maybe_sent:
        pl.when(condition)(copy.wait_send)

    for b in range(total):
        owner = owners[b]
        block = gathered[owner, jnp.where(table[0, owner] == b, 0, 1)]
        if b < values:
            out_values[b] = block
        else:
            out_keys[b - values] = block
    for copy in sent:
        copy.wait_send()


def store_kernel(*refs):
    half = (len(refs) - 1) // 2
    copies = [
        pltpu.make_async_copy(src, dst, refs[-1].at[i])
        for i, (src, dst) in enumerate(zip(refs[:half], refs[half:-1]))
    ]
    for copy in copies:
        copy.start()
    for copy in copies:
        copy.wait()


def on_device(value_grads, key_grads, owners, weights, left, right, left_root, right_root, second):
    dp_count = lax.axis_size("dp")
    mp_count = lax.axis_size("mp")
    capacity = weights.shape[2]
    values = value_grads.shape[1]
    side = value_grads.shape[2]
    share = key_grads.shape[2] // mp_count
    total = values + share
    outer = dp_count // 4
    f32, bf16 = jnp.float32, jnp.bfloat16
    block = (side, side)
    state = jax.ShapeDtypeStruct((1, 1, capacity) + block, f32)
    owner_ids = pltpu.with_memory_space_constraint(owners[:, 0], pltpu.HBM)
    hbm = pl.BlockSpec(memory_space=pl.ANY)
    vmem = pl.BlockSpec(memory_space=pltpu.VMEM)
    dma = pltpu.SemaphoreType.DMA
    peers = max(outer - 1, 1)
    others = max(mp_count - 1, 1)
    cut = side - side * 2 // 8
    out_cut = side - side * 2 // 8
    head, tail = (cut, side), (side - cut, side)
    results_shape = [state] * 4 + [
        jax.ShapeDtypeStruct((values,) + block, bf16),
        jax.ShapeDtypeStruct((share,) + block, bf16),
    ]
    results = pl.pallas_call(
        functools.partial(main_kernel, (dp_count, mp_count, values, share, capacity, cut, out_cut)),
        out_shape=results_shape,
        in_specs=[hbm] * 9,
        out_specs=[vmem] * 6,
        scratch_shapes=[
            pltpu.VMEM((dp_count, capacity) + block, bf16),
            pltpu.SMEM((total,), jnp.int32),
            pltpu.SMEM((2, dp_count), jnp.int32),
            pltpu.VMEM((total + 1,) + block, bf16),
            pltpu.VMEM((share,) + block, bf16),
            pltpu.VMEM((others, share) + block, bf16),
        ]
        + [pltpu.VMEM((capacity,) + block, f32)] * 6
        + [pltpu.VMEM((outer, 3, capacity) + head, bf16)] * 2
        + [pltpu.VMEM((peers, capacity) + head, bf16), pltpu.VMEM((outer, capacity) + head, bf16)]
        + [pltpu.VMEM((peers, 4, capacity) + tail, bf16), pltpu.VMEM((outer, 4, capacity) + tail, bf16)]
        + [pltpu.VMEM((3, capacity) + tail, bf16)] * 2
        + [pltpu.VMEM((capacity,) + block, f32)]
        + [dma((9,)), dma((others,)), dma((others,))]
        + [dma((outer, 3))] * 2
        + [dma((outer,))] * 4
        + [dma((3,))] * 2
        + [dma((peers,)), dma((outer, 3)), dma((3,)), dma((peers,)), dma((dp_count,)), dma((4,)), dma((outer,)), dma((2,)), pltpu.SemaphoreType.REGULAR],
        compiler_params=pltpu.CompilerParams(
            collective_id=0, has_side_effects=True, vmem_limit_bytes=32 * 1024 * 1024
        ),
    )(
        owner_ids,
        *(
            pltpu.with_memory_space_constraint(a, pltpu.HBM)
            for a in (value_grads, key_grads, weights, left, right, left_root, right_root, second)
        ),
    )
    return pl.pallas_call(
        store_kernel,
        out_shape=results_shape,
        in_specs=[hbm] * 6,
        out_specs=[hbm] * 6,
        scratch_shapes=[dma((6,))],
        compiler_params=pltpu.CompilerParams(vmem_limit_bytes=8 * 1024 * 1024),
    )(*results)


def solution(mesh):
    state = P("dp", "mp", None, None, None)
    return jax.shard_map(
        on_device,
        mesh=mesh,
        in_specs=(P("dp", "mp", None, None), state, P("mp", None)) + (state,) * 6,
        out_specs=(state,) * 4 + (P("mp", None, None),) * 2,
        check_vma=False,
    )
```
